256 devices in a mesh: lat: 16 (over y_lo, z), lon: 8 (over x, y_hi), comp: 2 (over core).
Axes of the slice: x: 4, y: 4 (y_hi: 2, y_lo: 2; y = y_hi * 2 + y_lo), z: 8, core: 2. Of those that a mesh axis runs over, the one named last changes fastest.
Arguments:
- atm_state: bfloat16 [2, 32, 2048, 384], P(None, 'lat', ('lon', 'comp')), may hold values from -6 to 6
- ocean_prev: bfloat16 [2, 32, 2048, 128], P(None, 'lat', ('lon', 'comp')), may hold values from -6 to 6
- land_sea: int32 [32, 2048], P('lat', ('lon', 'comp')), may hold values 0 or 1
- window_ids: int32 [32, 2048], P('lat', ('lon', 'comp')), may hold values from 0 to 2047, as said below
- conv_atm: float32 [2, 3, 3, 384], replicated, may hold values from -2 to 2
- attn_gain: float32 [2, 384], replicated, may hold values from 0.5 to 2
- qkv_matrix: bfloat16 [2, 384, 1152], replicated, may hold values from -0.3125 to 0.3125
- attn_scales: float32 [2, 6], replicated, may hold values from 4 to 32
- out_matrix: bfloat16 [2, 384, 384], replicated, may hold values from -0.3125 to 0.3125
- mlp_gain: float32 [2, 384], replicated, may hold values from 0.5 to 2
- member_in: float32 [2, 2, 384], replicated, may hold values from 0.5 to 2
- member_out: float32 [2, 2, 1536], replicated, may hold values from 0.5 to 2
- up_matrix: bfloat16 [2, 384, 1536], replicated, may hold values from -0.3125 to 0.3125
- down_matrix: bfloat16 [2, 1536, 384], replicated, may hold values from -0.15625 to 0.15625
- flux_matrix: bfloat16 [384, 128], replicated, may hold values from -0.3125 to 0.3125
- conv_ocean: float32 [3, 3, 3, 128], replicated, may hold values from -2 to 2
- point_matrix: bfloat16 [3, 128, 128], replicated, may hold values from -0.5 to 0.5
- ocean_gain: float32 [128], replicated, may hold values from 0.5 to 2
- ocean_qkv: bfloat16 [128, 384], replicated, may hold values from -0.5 to 0.5
- ocean_scale: float32 [2], replicated, may hold values from 4 to 32
- ocean_out: bfloat16 [128, 128], replicated, may hold values from -0.5 to 0.5
- seaside_return_matrix: bfloat16 [128, 384], replicated, may hold values from -0.5 to 0.5
Outputs:
- updated_airflow_field: bfloat16 [2, 32, 2048, 384], P(None, 'lat', ('lon', 'comp'))
- updated_seaside_channels: bfloat16 [2, 32, 2048, 128], P(None, 'lat', ('lon', 'comp'))
The draws below stay inside these ranges and needn't reach their ends.
Inputs may be any that keep to these rules, and one draw needn't show every extreme that they name: `land_sea`: 1 marks a sea column, 0 land. `window_ids`: along each latitude the value is the longitude of the first column of that column's window; it never falls along a row, every window lies inside an aligned run of 128 longitudes, and the last longitude of every row is a window of its own.
All inputs are finite; a program needn't handle non-finite values. No bound on the sum of `land_sea` on one device may be relied on, other than what follows from the above.
Results may differ from the reference program's by a relative error of at most 0.018.
Values may be sent and summed in bfloat16 or wider, within the bound.
No kernel may reach another device: no remote copies, remote signals or barrier semaphores. Data moves between devices by JAX's collectives and lax.ppermute only.
A program may use at most 64 MiB of HBM per device.

```python
import math
import jax
import jax.numpy as jnp
from jax import lax

WIDTH = 384
HEADS = 6
HIDDEN_SIZE = 1536
OCEAN = 128
OHEADS = 2
BLOCKS = 2
MEMBERS = 2
COLS_DEV = 128
NLAT = 32
NLON = 2048


def draw_window_ids(key, part):
    break_draw = jax.random.randint(key, (NLAT, NLON), 0, 12)
    lon_index = jnp.arange(NLON, dtype=jnp.int32)
    block_start = lon_index % COLS_DEV == 0
    last_column = lon_index == NLON - 1
    starts = (break_draw == 0) | block_start[None, :] | last_column[None, :]
    marked = jnp.where(starts, lon_index[None, :], 0)
    return lax.cummax(marked, axis=1).astype(jnp.int32)


def place_ends(values, rng, smallest, largest):
    spot = [jax.random.randint(jax.random.fold_in(rng, axis), (), 0, length) for axis, length in enumerate(values.shape)]
    widest = values.shape.index(max(values.shape))
    beside = spot[:widest] + [(spot[widest] + 1) % values.shape[widest]] + spot[widest + 1:]
    return values.at[tuple(spot)].set(smallest).at[tuple(beside)].set(largest)


def levels(key, extent, pieces, smallest, high):
    def one(axis_at, parts):
        draws = jax.random.uniform(jax.random.fold_in(jax.random.fold_in(key, 6), axis_at), (parts,), jnp.float32, smallest / len(pieces), high / len(pieces))
        return jnp.repeat(jnp.exp(draws), extent[axis_at] // parts).reshape((-1,) + (1,) * (len(extent) - axis_at - 1))

    factor_of = one(*pieces[0])
    for cut in pieces[1:]:
        factor_of = factor_of * one(*cut)
    return factor_of


def bell_draw(rng, dims, scale, reach, split=(), kind=jnp.bfloat16):
    array = jax.random.normal(rng, dims, jnp.float32) * scale
    if len(split) > 0:
        array = levels(rng, dims, split, -0.22, 0.18) * array
    return jnp.clip(array, min=-reach, max=reach).astype(kind)


def setup_inputs(seed: int = 0) -> dict:
    keys = jax.random.split(jax.random.key(seed), 23)
    return {
        "atm_state": bell_draw(keys[0], (MEMBERS, NLAT, NLON, WIDTH), 1.0, 6.0, ((1, 16), (2, 16))),
        "ocean_prev": bell_draw(keys[1], (MEMBERS, NLAT, NLON, OCEAN), 1.0, 6.0, ((1, 16), (2, 16))),
        "land_sea": place_ends((jax.random.randint(keys[2], (NLAT, NLON), 0, 10) < 7).astype(jnp.int32), jax.random.fold_in(keys[2], 1), 0, 1),
        "window_ids": draw_window_ids(jax.random.fold_in(keys[22], 71), 0),
        "conv_atm": bell_draw(keys[4], (BLOCKS, 3, 3, WIDTH), 0.35, 2.0, (), jnp.float32),
        "attn_gain": jnp.clip(jnp.exp(jax.random.uniform(keys[5], (BLOCKS, WIDTH), jnp.float32, math.log(0.5), math.log(2.0))), 0.5, 2.0),
        "qkv_matrix": bell_draw(keys[6], (BLOCKS, WIDTH, 3 * WIDTH), WIDTH ** -0.5, 0.3125),
        "attn_scales": jnp.clip(jnp.exp(jax.random.uniform(keys[7], (BLOCKS, HEADS), jnp.float32, math.log(4.0), math.log(32.0))), 4.0, 32.0),
        "out_matrix": bell_draw(keys[8], (BLOCKS, WIDTH, WIDTH), WIDTH ** -0.5, 0.3125),
        "mlp_gain": jnp.clip(jnp.exp(jax.random.uniform(keys[9], (BLOCKS, WIDTH), jnp.float32, math.log(0.5), math.log(2.0))), 0.5, 2.0),
        "member_in": jnp.clip(jnp.exp(jax.random.uniform(keys[10], (BLOCKS, MEMBERS, WIDTH), jnp.float32, math.log(0.5), math.log(2.0))), 0.5, 2.0),
        "member_out": jnp.clip(jnp.exp(jax.random.uniform(keys[11], (BLOCKS, MEMBERS, HIDDEN_SIZE), jnp.float32, math.log(0.5), math.log(2.0))), 0.5, 2.0),
        "up_matrix": bell_draw(keys[12], (BLOCKS, WIDTH, HIDDEN_SIZE), WIDTH ** -0.5, 0.3125),
        "down_matrix": bell_draw(keys[13], (BLOCKS, HIDDEN_SIZE, WIDTH), HIDDEN_SIZE ** -0.5, 0.15625),
        "flux_matrix": bell_draw(keys[14], (WIDTH, OCEAN), WIDTH ** -0.5, 0.3125),
        "conv_ocean": bell_draw(keys[15], (3, 3, 3, OCEAN), 0.35, 2.0, (), jnp.float32),
        "point_matrix": bell_draw(keys[16], (3, OCEAN, OCEAN), OCEAN ** -0.5, 0.5),
        "ocean_gain": jnp.clip(jnp.exp(jax.random.uniform(keys[17], (OCEAN,), jnp.float32, math.log(0.5), math.log(2.0))), 0.5, 2.0),
        "ocean_qkv": bell_draw(keys[18], (OCEAN, 3 * OCEAN), OCEAN ** -0.5, 0.5),
        "ocean_scale": jnp.clip(jnp.exp(jax.random.uniform(keys[19], (OHEADS,), jnp.float32, math.log(4.0), math.log(32.0))), 4.0, 32.0),
        "ocean_out": bell_draw(keys[20], (OCEAN, OCEAN), OCEAN ** -0.5, 0.5),
        "seaside_return_matrix": bell_draw(keys[21], (OCEAN, WIDTH), OCEAN ** -0.5, 0.5),
    }


NORM_EPS = 1e-05
UNIT_EPS = 1e-06

def damped_model_field(values_in):
    return lax.optimization_barrier(values_in.astype(jnp.bfloat16))

def smooth(values_in):
    return jax.nn.gelu(values_in, approximate=False)

def layer_norm(values_in, gain_vector):
    widened = values_in.astype(jnp.float32)
    centred = widened - lax.optimization_barrier(jnp.mean(widened, axis=-1, keepdims=True))
    spread = lax.optimization_barrier(jnp.mean(centred * centred, axis=-1, keepdims=True))
    return centred * lax.rsqrt(spread + NORM_EPS) * gain_vector

def unit_heads(projected, head_count):
    shaped = projected.reshape(projected.shape[:-1] + (head_count, projected.shape[-1] // head_count))
    shaped = shaped * lax.rsqrt(lax.optimization_barrier(jnp.mean(shaped * shaped, axis=-1, keepdims=True)) + UNIT_EPS)
    return damped_model_field(shaped.reshape(projected.shape))

def nine_taps(padded, kernel):
    row_count = padded.shape[1] - 2
    col_count = padded.shape[2] - 2
    accum = jnp.zeros((padded.shape[0], row_count, col_count, padded.shape[3]), jnp.float32)
    for lat_shift in range(3):
        for lon_shift in range(3):
            window = padded[:, lat_shift:lat_shift + row_count, lon_shift:lon_shift + col_count]
            accum = accum + window.astype(jnp.float32) * kernel[lat_shift, lon_shift]
    return accum

def global_conv(values_in, kernel):
    padded = jnp.pad(values_in, ((0, 0), (1, 1), (0, 0), (0, 0)))
    padded = jnp.concatenate([padded[:, :, -1:], padded, padded[:, :, :1]], axis=2)
    return nine_taps(padded, kernel)

def window_attend(query_units, key_units, value_rows, window_ids, head_scale):
    members, row_count, length, channels = query_units.shape
    head_count = head_scale.shape[0]
    head_dim = channels // head_count
    blocks = length // COLS_DEV
    shape_six = (members, row_count, blocks, COLS_DEV, head_count, head_dim)
    query_six = query_units.reshape(shape_six).astype(jnp.float32)
    key_six = key_units.reshape(shape_six).astype(jnp.float32)
    value_six = value_rows.reshape(shape_six).astype(jnp.float32)
    id_blocks = window_ids.reshape(row_count, blocks, COLS_DEV)
    same_window = id_blocks[:, :, :, None] == id_blocks[:, :, None, :]
    scores = jnp.einsum('mrbqhd,mrbkhd->mrbhqk', query_six, key_six) * (head_scale / head_dim)[:, None, None]
    exp_terms = jnp.where(same_window[None, :, :, None], jnp.exp(scores), 0.0)
    denominator = lax.optimization_barrier(jnp.sum(exp_terms, axis=-1))
    numerator = jnp.einsum('mrbhqk,mrbkhd->mrbqhd', damped_model_field(exp_terms).astype(jnp.float32), value_six)
    result = numerator / jnp.transpose(denominator, (0, 1, 2, 4, 3))[..., None]
    return damped_model_field(result.reshape(members, row_count, length, channels))

def token_section(mixed_state, window_ids, attn_gain, qkv_matrix, attn_scales, out_matrix, mlp_gain, scale_in, scale_out, up_matrix, down_matrix):
    normed = damped_model_field(layer_norm(mixed_state, attn_gain))
    projected = jnp.dot(normed, qkv_matrix, preferred_element_type=jnp.float32)
    query_units = unit_heads(projected[..., :WIDTH], HEADS)
    key_units = unit_heads(projected[..., WIDTH:2 * WIDTH], HEADS)
    value_rows = damped_model_field(projected[..., 2 * WIDTH:])
    attended = window_attend(query_units, key_units, value_rows, window_ids, attn_scales)
    after_attn = damped_model_field(mixed_state.astype(jnp.float32) + jnp.dot(attended, out_matrix, preferred_element_type=jnp.float32))
    scaled = damped_model_field(layer_norm(after_attn, mlp_gain) * scale_in[:, None, None, :])
    lifted_channel_values = jnp.dot(scaled, up_matrix, preferred_element_type=jnp.float32) * scale_out[:, None, None, :]
    activated = damped_model_field(smooth(lifted_channel_values))
    return damped_model_field(after_attn.astype(jnp.float32) + jnp.dot(activated, down_matrix, preferred_element_type=jnp.float32))

def pool_pairs(values_in):
    members, row_count, col_count, channels = values_in.shape
    shaped = values_in.astype(jnp.float32).reshape(members, row_count // 2, 2, col_count // 2, 2, channels)
    return lax.optimization_barrier(jnp.mean(shaped, axis=(2, 4)))

def upsample(coarse):
    members, row_count, col_count, channels = coarse.shape
    spread_out = jnp.broadcast_to(coarse[:, :, None, :, None, :], (members, row_count, 2, col_count, 2, channels))
    return spread_out.reshape(members, 2 * row_count, 2 * col_count, channels)

def lat_terms(query_units, key_units, value_rows, head_scale):
    head_count = head_scale.shape[0]
    head_dim = query_units.shape[-1] // head_count
    query_five = query_units.reshape(query_units.shape[:-1] + (head_count, head_dim)).astype(jnp.float32)
    key_five = key_units.reshape(key_units.shape[:-1] + (head_count, head_dim)).astype(jnp.float32)
    value_five = value_rows.reshape(key_units.shape[:-1] + (head_count, head_dim)).astype(jnp.float32)
    scores = jnp.einsum('mijhd,mkjhd->mhikj', query_five, key_five) * (head_scale / head_dim)[None, :, None, None, None]
    exp_terms = jnp.exp(scores)
    denominator = lax.optimization_barrier(jnp.sum(exp_terms, axis=3))
    numerator = jnp.einsum('mhikj,mkjhd->mijhd', damped_model_field(exp_terms).astype(jnp.float32), value_five)
    return (numerator, denominator)

def finish_heads(numerator, denominator):
    result = numerator / jnp.transpose(denominator, (0, 2, 3, 1))[..., None]
    return damped_model_field(result.reshape(result.shape[:3] + (result.shape[3] * result.shape[4],)))

def ocean_trunk(marine_starting_field, conv_ocean, point_matrix, ocean_gain, ocean_qkv, ocean_scale, ocean_out):
    act_first = damped_model_field(global_conv(marine_starting_field, conv_ocean[0]))
    fine_first = damped_model_field(smooth(jnp.dot(act_first, point_matrix[0], preferred_element_type=jnp.float32)))
    coarse_start = damped_model_field(pool_pairs(fine_first))
    act_second = damped_model_field(global_conv(coarse_start, conv_ocean[1]))
    coarse_first = damped_model_field(smooth(jnp.dot(act_second, point_matrix[1], preferred_element_type=jnp.float32)))
    normed = damped_model_field(layer_norm(coarse_first, ocean_gain))
    projected = jnp.dot(normed, ocean_qkv, preferred_element_type=jnp.float32)
    query_units = unit_heads(projected[..., :OCEAN], OHEADS)
    key_units = unit_heads(projected[..., OCEAN:2 * OCEAN], OHEADS)
    value_rows = damped_model_field(projected[..., 2 * OCEAN:])
    numerator, denominator = lat_terms(query_units, key_units, value_rows, ocean_scale)
    attended = finish_heads(numerator, denominator)
    coarse_next = damped_model_field(coarse_first.astype(jnp.float32) + jnp.dot(attended, ocean_out, preferred_element_type=jnp.float32))
    merged = damped_model_field(fine_first.astype(jnp.float32) + upsample(coarse_next).astype(jnp.float32))
    return damped_model_field(global_conv(merged, conv_ocean[2]))

def reference(atm_state, ocean_prev, land_sea, window_ids, conv_atm, attn_gain, qkv_matrix, attn_scales, out_matrix, mlp_gain, member_in, member_out, up_matrix, down_matrix, flux_matrix, conv_ocean, point_matrix, ocean_gain, ocean_qkv, ocean_scale, ocean_out, seaside_return_matrix):
    current_model_field = atm_state
    for block_index in range(BLOCKS):
        mixed_state = damped_model_field(current_model_field.astype(jnp.float32) + global_conv(current_model_field, conv_atm[block_index]))

        def per_row(row_args):
            row_state, row_ids = row_args
            return token_section(row_state, row_ids, attn_gain[block_index], qkv_matrix[block_index], attn_scales[block_index], out_matrix[block_index], mlp_gain[block_index], member_in[block_index], member_out[block_index], up_matrix[block_index], down_matrix[block_index])
        rows_out = lax.map(per_row, (jnp.moveaxis(mixed_state, 1, 0)[:, :, None], window_ids[:, None, :]))
        current_model_field = jnp.moveaxis(rows_out[:, :, 0], 0, 1)
    marine_grid_indicator = land_sea.astype(jnp.float32)[None, :, :, None]
    flux_terms = jnp.dot(current_model_field, flux_matrix, preferred_element_type=jnp.float32)
    marine_starting_field = damped_model_field(marine_grid_indicator * (ocean_prev.astype(jnp.float32) + flux_terms))
    act_last = ocean_trunk(marine_starting_field, conv_ocean, point_matrix, ocean_gain, ocean_qkv, ocean_scale, ocean_out)
    lifted_channel_values = smooth(jnp.dot(act_last, point_matrix[2], preferred_element_type=jnp.float32))
    updated_seaside_channels = damped_model_field(marine_grid_indicator * (marine_starting_field.astype(jnp.float32) + lifted_channel_values))
    updated_airflow_field = damped_model_field(current_model_field.astype(jnp.float32) + marine_grid_indicator * jnp.dot(updated_seaside_channels, seaside_return_matrix, preferred_element_type=jnp.float32))
    return (updated_airflow_field, updated_seaside_channels)
```

```python
import jax
import jax.numpy as jnp
from jax import lax
from jax.experimental import pallas as pl
from jax.experimental.pallas import tpu as pltpu
from jax.sharding import PartitionSpec as P

WIDTH = 384
HEADS = 6
HIDDEN = 1536
OCEAN = 128
BLOCKS = 2
COLS = 128
NORM_EPS = 1e-05
UNIT_EPS = 1e-06
LOG2E = 1.4426950408889634
F32 = jnp.float32
BF16 = jnp.bfloat16
VM = pl.BlockSpec(memory_space=pltpu.VMEM)
SM = pl.BlockSpec(memory_space=pltpu.SMEM)
ANY = pl.BlockSpec(memory_space=pl.ANY)


def dot(a, b):
    return jnp.dot(a, b, preferred_element_type=F32)


def dot_t(a, b):
    return lax.dot_general(a, b, (((1,), (1,)), ((), ())), preferred_element_type=F32)


def gelu(v):
    mag = jnp.abs(v)
    t = 1.0 / (mag * (0.3275911 * 0.7071067811865476) + 1.0)
    poly = t * (0.5 * 1.061405429) + (0.5 * -1.453152027)
    poly = poly * t + (0.5 * 1.421413741)
    poly = poly * t + (0.5 * -0.284496736)
    poly = poly * t + (0.5 * 0.254829592)
    tail = jnp.exp2(v * v * (-0.5 * LOG2E))
    return jnp.maximum(v, 0.0) - (mag * (poly * t)) * tail


def norm_rows(x, gain):
    centred = x - jnp.mean(x, axis=-1, keepdims=True)
    spread = jnp.mean(centred * centred, axis=-1, keepdims=True)
    return centred * lax.rsqrt(spread + NORM_EPS) * gain


def head_mean(size):
    row = lax.broadcasted_iota(jnp.int32, (size, size), 0) // 64
    col = lax.broadcasted_iota(jnp.int32, (size, size), 1) // 64
    return jnp.where(row == col, 1.0 / 64.0, 0.0).astype(BF16)


def unit(p, mean_matrix):
    square = (p * p).astype(BF16)
    return (p * lax.rsqrt(dot(square, mean_matrix) + UNIT_EPS)).astype(BF16)


def pair_attend(q, k, v, mask, scale_even, scale_odd):
    low = lax.broadcasted_iota(jnp.int32, q.shape, 1) < 64
    zero = jnp.zeros_like(q)
    stacked = jnp.concatenate([jnp.where(low, q, zero), jnp.where(low, zero, q)], axis=0)
    scores = dot_t(stacked, k)
    rows = q.shape[0]
    even = jnp.exp2(scores[:rows] * scale_even) * mask
    odd = jnp.exp2(scores[rows:] * scale_odd) * mask
    terms = jnp.concatenate([even, odd], axis=0).astype(BF16)
    ext = jnp.concatenate([v, jnp.ones_like(v)], axis=1)
    sums = dot(terms, ext)
    number = jnp.where(low, sums[:rows, :128], sums[rows:, :128])
    denom = jnp.where(low, sums[:rows, 128:], sums[rows:, 128:])
    return (number / denom).astype(BF16)


def shift_cols(t, step, axis):
    return pltpu.roll(t, step % t.shape[axis], axis)


def conv_kernel(block, top_ref, bot_ref, up_ref, down_ref, k_ref, part_ref, right_ref, left_ref):
    lat = lax.axis_index("lat")
    last = lax.axis_size("lat") - 1
    has_up = (lat > 0).astype(F32)
    has_down = (lat < last).astype(F32)
    first_col = lax.broadcasted_iota(jnp.int32, (COLS, WIDTH), 0) == 0
    final_col = lax.broadcasted_iota(jnp.int32, (COLS, WIDTH), 0) == COLS - 1

    def tap(i, j):
        return k_ref[block, i, j : j + 1, :]

    for m in range(2):
        rows = [
            up_ref[m].astype(F32) * has_up,
            top_ref[m].astype(F32),
            bot_ref[m].astype(F32),
            down_ref[m].astype(F32) * has_down,
        ]
        for r in range(2):
            a, b, c = rows[r : r + 3]
            mid = tap(0, 1) * a + (tap(1, 1) + 1.0) * b + tap(2, 1) * c
            west = tap(0, 0) * a + tap(1, 0) * b + tap(2, 0) * c
            east = tap(0, 2) * a + tap(1, 2) * b + tap(2, 2) * c
            right_ref[2 * m + r : 2 * m + r + 1, :] = west[COLS - 1 :, :]
            left_ref[2 * m + r : 2 * m + r + 1, :] = east[:1, :]
            part_ref[m, r] = (
                mid
                + jnp.where(first_col, 0.0, shift_cols(west, 1, 0))
                + jnp.where(final_col, 0.0, shift_cols(east, -1, 0))
            )


def conv_call(block, top, bot, up, down, kernels):
    shape = (2, 2, COLS, WIDTH)
    return pl.pallas_call(
        lambda *refs: conv_kernel(block, *refs),
        out_shape=(
            jax.ShapeDtypeStruct(shape, F32),
            jax.ShapeDtypeStruct((4, WIDTH), F32),
            jax.ShapeDtypeStruct((4, WIDTH), F32),
        ),
        in_specs=[VM] * 5,
        out_specs=(VM,) * 3,
        name=f"conv_{block}",
    )(top, bot, up, down, kernels)


def block_body(block, scale_ref, part_ref, west_ref, east_ref, mask_ref, gain_ref, mlp_gain_ref,
               min_ref, mout_ref, weights, store):
    qkv_ref, out_ref, up_ref, down_ref = weights
    first_col = lax.broadcasted_iota(jnp.int32, (COLS, WIDTH), 0) == 0
    final_col = lax.broadcasted_iota(jnp.int32, (COLS, WIDTH), 0) == COLS - 1
    mean_matrix = head_mean(256)
    waits = []
    for m in range(2):
        rows = []
        for r in range(2):
            i = 2 * m + r
            x = part_ref[m, r]
            x = x + jnp.where(first_col, west_ref[i : i + 1, :], 0.0)
            x = x + jnp.where(final_col, east_ref[i : i + 1, :], 0.0)
            rows.append(x.astype(BF16))
        mixed = jnp.concatenate(rows, axis=0).astype(F32)
        normed = norm_rows(mixed, gain_ref[block : block + 1, :]).astype(BF16)
        qkv = dot(normed, qkv_ref())
        units = [unit(qkv[:, 256 * i : 256 * i + 256], mean_matrix) for i in range(3)]
        value = qkv[:, 2 * WIDTH :].astype(BF16)

        def lanes(j):
            return units[j // 2][:, 128 * (j % 2) : 128 * (j % 2) + 128]

        row_out = []
        for r in range(2):
            at = slice(COLS * r, COLS * r + COLS)
            pieces = []
            for j in range(3):
                pieces.append(
                    pair_attend(
                        lanes(j)[at],
                        lanes(3 + j)[at],
                        value[at, 128 * j : 128 * j + 128],
                        mask_ref[r],
                        scale_ref[block, 2 * j] * (LOG2E / 64),
                        scale_ref[block, 2 * j + 1] * (LOG2E / 64),
                    )
                )
            row_out.append(jnp.concatenate(pieces, axis=1))
        attended = jnp.concatenate(row_out, axis=0)
        after = (mixed + dot(attended, out_ref())).astype(BF16)
        after_f = after.astype(F32)
        gain = mlp_gain_ref[block : block + 1, :] * min_ref[block, m : m + 1, :]
        scaled = norm_rows(after_f, gain).astype(BF16)
        total = after_f
        step = 512
        for h in range(0, HIDDEN, step):
            lifted = dot(scaled, up_ref(h, step)) * mout_ref[block, m : m + 1, h : h + step]
            total = total + dot(gelu(lifted).astype(BF16), down_ref(h, step))
        store(m, total.astype(BF16))


def weight_getters(block, hbm, bufs, sems):
    copies = [
        pltpu.make_async_copy(src.at[block], buf, sems.at[i])
        for i, (src, buf) in enumerate(zip(hbm, bufs))
    ]
    for copy in copies:
        copy.start()
    done = set()

    def ready(i):
        if i not in done:
            copies[i].wait()
            done.add(i)

    def qkv():
        ready(0)
        return bufs[0][...]

    def out():
        ready(1)
        return bufs[1][...]

    def up(h, n):
        ready(2)
        return bufs[2][:, h : h + n]

    def down(h, n):
        ready(3)
        return bufs[3][h : h + n, :]

    return qkv, out, up, down


WEIGHT_SCRATCH = [
    pltpu.VMEM((WIDTH, 3 * WIDTH), BF16),
    pltpu.VMEM((WIDTH, WIDTH), BF16),
    pltpu.VMEM((WIDTH, HIDDEN), BF16),
    pltpu.VMEM((HIDDEN, WIDTH), BF16),
    pltpu.SemaphoreType.DMA((4,)),
]


def first_kernel(scale_ref, part_ref, west_ref, east_ref, mask_ref, gain_ref, mlp_gain_ref, min_ref,
                 mout_ref, qkv_h, out_h, up_h, down_h, top_ref, bot_ref, b0, b1, b2, b3, sems):
    weights = weight_getters(0, (qkv_h, out_h, up_h, down_h), (b0, b1, b2, b3), sems)

    def store(m, value):
        top_ref[m] = value[:COLS]
        bot_ref[m] = value[COLS:]

    block_body(0, scale_ref, part_ref, west_ref, east_ref, mask_ref, gain_ref, mlp_gain_ref,
               min_ref, mout_ref, weights, store)


def second_kernel(scale_ref, part_ref, west_ref, east_ref, mask_ref, gain_ref, mlp_gain_ref, min_ref,
                  mout_ref, qkv_h, out_h, up_h, down_h, prev_ref, sea_ref, flux_ref,
                  cur_ref, start_ref, b0, b1, b2, b3, sems):
    weights = weight_getters(1, (qkv_h, out_h, up_h, down_h), (b0, b1, b2, b3), sems)

    def store(m, value):
        flux = dot(value, flux_ref[...])
        for r in range(2):
            at = slice(COLS * r, COLS * r + COLS)
            cur_ref[m, r] = value[at]
            start = sea_ref[r] * (prev_ref[m, r].astype(F32) + flux[at])
            start_ref[:, 2 * m + r] = start.astype(BF16).reshape(16, 8, OCEAN)

    block_body(1, scale_ref, part_ref, west_ref, east_ref, mask_ref, gain_ref, mlp_gain_ref,
               min_ref, mout_ref, weights, store)


def first_call(*args):
    row = jax.ShapeDtypeStruct((2, COLS, WIDTH), BF16)
    return pl.pallas_call(
        first_kernel,
        out_shape=(row, row),
        in_specs=[SM] + [VM] * 8 + [ANY] * 4,
        out_specs=(VM, VM),
        scratch_shapes=WEIGHT_SCRATCH,
        name="block_0",
    )(*args)


def second_call(*args):
    return pl.pallas_call(
        second_kernel,
        out_shape=(
            jax.ShapeDtypeStruct((2, 2, COLS, WIDTH), BF16),
            jax.ShapeDtypeStruct((16, 4, 8, OCEAN), BF16),
        ),
        in_specs=[SM] + [VM] * 8 + [ANY] * 4 + [VM] * 3,
        out_specs=(VM, VM),
        scratch_shapes=WEIGHT_SCRATCH,
        name="block_1",
    )(*args)


def taps3(field, k_ref, index):
    zero = jnp.zeros_like(field[:1])
    above = jnp.concatenate([zero, field[:-1]], axis=0)
    below = jnp.concatenate([field[1:], zero], axis=0)

    def column(j):
        return (
            k_ref[index, 0, j : j + 1, :] * above
            + k_ref[index, 1, j : j + 1, :] * field
            + k_ref[index, 2, j : j + 1, :] * below
        )

    return column(1) + shift_cols(column(0), 1, 1) + shift_cols(column(2), -1, 1)


def ocean_kernel(scale_ref, own_ref, west_ref, east_ref, k_ref, point_ref, gain_ref, qkv_ref,
                 out_ref, last_ref, pool_ref, wide_ref):
    mean_matrix = head_mean(128)
    row = lax.broadcasted_iota(jnp.int32, (128, 128), 0) % 8
    col = lax.broadcasted_iota(jnp.int32, (128, 128), 1) % 8
    mask = jnp.where(row == col, 1.0, 0.0)
    wide_ref[...] = jnp.zeros_like(wide_ref)
    for m in range(2):
        def rows_of(ref):
            even = ref[:, 2 * m].astype(F32)[:, None]
            odd = ref[:, 2 * m + 1].astype(F32)[:, None]
            return jnp.concatenate([even, odd], axis=1).reshape(32, 8, OCEAN)

        field = jnp.concatenate([rows_of(west_ref), rows_of(own_ref), rows_of(east_ref)], axis=1)
        act = taps3(field, k_ref, 0).astype(BF16).reshape(32 * 24, OCEAN)
        fine = gelu(dot(act, point_ref[0])).astype(BF16).astype(F32)
        fine4 = fine.reshape(16, 2, 24, OCEAN)
        pool_ref[...] = (fine4[:, 0] + fine4[:, 1]).reshape(16 * 24, OCEAN)
        coarse = []
        for i in range(16):
            coarse.append(
                pool_ref[pl.ds(24 * i + 4, 8, stride=2), :]
                + pool_ref[pl.ds(24 * i + 5, 8, stride=2), :]
            )
        coarse = (jnp.concatenate(coarse, axis=0) * 0.25).astype(BF16).astype(F32)
        act = taps3(coarse.reshape(16, 8, OCEAN), k_ref, 1).astype(BF16).reshape(128, OCEAN)
        first = gelu(dot(act, point_ref[1])).astype(BF16).astype(F32)
        normed = norm_rows(first, gain_ref[...]).astype(BF16)
        qkv = dot(normed, qkv_ref[...])
        attended = pair_attend(
            unit(qkv[:, :128], mean_matrix),
            unit(qkv[:, 128:256], mean_matrix),
            qkv[:, 256:].astype(BF16),
            mask,
            scale_ref[0] * (LOG2E / 64),
            scale_ref[1] * (LOG2E / 64),
        )
        following = (first + dot(attended, out_ref[...])).astype(BF16).astype(F32)
        for i in range(16):
            piece = following[8 * i : 8 * i + 8]
            wide_ref[pl.ds(24 * i + 4, 8, stride=2), :] = piece
            wide_ref[pl.ds(24 * i + 5, 8, stride=2), :] = piece
        spread = wide_ref[...].reshape(16, 1, 24, OCEAN)
        merged = (fine4 + spread).astype(BF16).astype(F32).reshape(32, 24, OCEAN)
        act = taps3(merged, k_ref, 2)[:, 8:16].astype(BF16).reshape(16, 2, 8, OCEAN)
        last_ref[:, 2 * m] = act[:, 0]
        last_ref[:, 2 * m + 1] = act[:, 1]


def ocean_call(*args):
    return pl.pallas_call(
        ocean_kernel,
        out_shape=jax.ShapeDtypeStruct((16, 4, 8, OCEAN), BF16),
        in_specs=[SM] + [VM] * 8,
        out_specs=VM,
        scratch_shapes=[pltpu.VMEM((16 * 24, OCEAN), F32), pltpu.VMEM((16 * 24, OCEAN), F32)],
        name="ocean",
    )(*args)


def final_kernel(last_ref, start_ref, cur_ref, sea_ref, point_ref, return_ref, air_ref, water_ref):
    for m in range(2):
        for r in range(2):
            i = 2 * m + r
            act = last_ref[:, i].reshape(COLS, OCEAN)
            lifted = gelu(dot(act, point_ref[2]))
            sea = sea_ref[r]
            water = (sea * (start_ref[:, i].reshape(COLS, OCEAN).astype(F32) + lifted)).astype(BF16)
            water_ref[m, r] = water
            back = dot(water, return_ref[...])
            sea3 = jnp.concatenate([sea, sea, sea], axis=1)
            air_ref[m, r] = (cur_ref[m, r].astype(F32) + sea3 * back).astype(BF16)


def final_call(*args):
    return pl.pallas_call(
        final_kernel,
        out_shape=(
            jax.ShapeDtypeStruct((2, 2, COLS, WIDTH), BF16),
            jax.ShapeDtypeStruct((2, 2, COLS, OCEAN), BF16),
        ),
        in_specs=[VM] * 6,
        out_specs=(VM, VM),
        name="final",
    )(*args)


LON = ("lon", "comp")


def ring(count, step):
    return [(i, (i + step) % count) for i in range(count)]


def group_ring(step):
    lats = lax.axis_size("lat")
    sectors = lax.axis_size("lon") * lax.axis_size("comp")
    total = lats * sectors
    pairs = []
    for g in range(total):
        t = (g + step) % total
        pairs.append(((g % lats) * sectors + g // lats, (t % lats) * sectors + t // lats))
    return pairs


def mix(block, top, bot, kernels):
    lats = lax.axis_size("lat")
    sectors = lax.axis_size("lon") * lax.axis_size("comp")
    up = lax.ppermute(bot, "lat", ring(lats, 1))
    down = lax.ppermute(top, "lat", ring(lats, -1))
    part, right, left = conv_call(block, top, bot, up, down, kernels)
    west = lax.ppermute(right, LON, ring(sectors, 1))
    east = lax.ppermute(left, LON, ring(sectors, -1))
    return part, west, east


def per_device(atm_state, ocean_prev, land_sea, window_ids, conv_atm, attn_gain, qkv_matrix,
               attn_scales, out_matrix, mlp_gain, member_in, member_out, up_matrix, down_matrix,
               flux_matrix, conv_ocean, point_matrix, ocean_gain, ocean_qkv, ocean_scale, ocean_out,
               seaside_return_matrix):
    mask = (window_ids[:, :, None] == window_ids[:, None, :]).astype(F32)
    sea = jnp.broadcast_to(land_sea.astype(F32)[:, :, None], (2, COLS, OCEAN))
    small = (attn_gain, mlp_gain, member_in, member_out)
    weights = (qkv_matrix, out_matrix, up_matrix, down_matrix)

    part, west, east = mix(0, atm_state[:, 0], atm_state[:, 1], conv_atm)
    top, bot = first_call(attn_scales, part, west, east, mask, *small, *weights)
    part, west, east = mix(1, top, bot, conv_atm)
    current, start = second_call(
        attn_scales, part, west, east, mask, *small, *weights, ocean_prev, sea, flux_matrix
    )
    own = lax.all_to_all(start, "lat", 0, 0)
    axes = ("lat",) + LON
    west = lax.ppermute(own, axes, group_ring(1))
    east = lax.ppermute(own, axes, group_ring(-1))
    last = ocean_call(ocean_scale, own, west, east, conv_ocean, point_matrix,
                      ocean_gain[None, :], ocean_qkv, ocean_out)
    last = lax.all_to_all(last, "lat", 0, 0)
    return final_call(last, start, current, sea, point_matrix, seaside_return_matrix)


def solution(mesh):
    field = P(None, "lat", LON, None)
    column = P("lat", LON)
    return jax.shard_map(
        per_device,
        mesh=mesh,
        in_specs=(field, field, column, column) + (P(),) * 18,
        out_specs=(field, field),
        check_vma=False,
    )
```

```python
import jax
import jax.numpy as jnp
from jax import lax
from jax.experimental import pallas as pl
from jax.experimental.pallas import tpu as pltpu
from jax.sharding import PartitionSpec as P

WIDTH = 384
HEADS = 6
HIDDEN = 1536
OCEAN = 128
BLOCKS = 2
COLS = 128
NORM_EPS = 1e-05
UNIT_EPS = 1e-06
LOG2E = 1.4426950408889634
F32 = jnp.float32
BF16 = jnp.bfloat16
VM = pl.BlockSpec(memory_space=pltpu.VMEM)
SM = pl.BlockSpec(memory_space=pltpu.SMEM)
ANY = pl.BlockSpec(memory_space=pl.ANY)
PARAMS = pltpu.CompilerParams(vmem_limit_bytes=20 * 1024 * 1024)


def near(*arrays):
    return tuple(pltpu.with_memory_space_constraint(a, pltpu.VMEM) for a in arrays)


def dot(a, b):
    return jnp.dot(a, b, preferred_element_type=F32)


def dot_t(a, b):
    return lax.dot_general(a, b, (((1,), (1,)), ((), ())), preferred_element_type=F32)


def gelu(v):
    mag = jnp.abs(v)
    t = 1.0 / (mag * (0.3275911 * 0.7071067811865476) + 1.0)
    poly = t * (0.5 * 1.061405429) + (0.5 * -1.453152027)
    poly = poly * t + (0.5 * 1.421413741)
    poly = poly * t + (0.5 * -0.284496736)
    poly = poly * t + (0.5 * 0.254829592)
    tail = jnp.exp2(v * v * (-0.5 * LOG2E))
    return jnp.maximum(v, 0.0) - (mag * (poly * t)) * tail


def norm_rows(x, gain):
    centred = x - jnp.mean(x, axis=-1, keepdims=True)
    spread = jnp.mean(centred * centred, axis=-1, keepdims=True)
    return centred * lax.rsqrt(spread + NORM_EPS) * gain


def head_mean(size):
    row = lax.broadcasted_iota(jnp.int32, (size, size), 0) // 64
    col = lax.broadcasted_iota(jnp.int32, (size, size), 1) // 64
    return jnp.where(row == col, 1.0 / 64.0, 0.0).astype(BF16)


def unit(p, mean_matrix):
    square = (p * p).astype(BF16)
    return (p * lax.rsqrt(dot(square, mean_matrix) + UNIT_EPS)).astype(BF16)


def pair_attend(q, k, v, mask, scale_even, scale_odd):
    low = lax.broadcasted_iota(jnp.int32, q.shape, 1) < 64
    zero = jnp.zeros_like(q)
    stacked = jnp.concatenate([jnp.where(low, q, zero), jnp.where(low, zero, q)], axis=0)
    scores = dot_t(stacked, k)
    rows = q.shape[0]
    even = jnp.exp2(scores[:rows] * scale_even) * mask
    odd = jnp.exp2(scores[rows:] * scale_odd) * mask
    terms = jnp.concatenate([even, odd], axis=0).astype(BF16)
    ext = jnp.concatenate([v, jnp.ones_like(v)], axis=1)
    sums = dot(terms, ext)
    number = jnp.where(low, sums[:rows, :128], sums[rows:, :128])
    denom = jnp.where(low, sums[:rows, 128:], sums[rows:, 128:])
    return (number / denom).astype(BF16)


def shift_cols(t, step, axis):
    return pltpu.roll(t, step % t.shape[axis], axis)


def conv_kernel(block, top_ref, bot_ref, up_ref, down_ref, k_ref, part_ref, mate_ref, far_ref):
    lat = lax.axis_index("lat")
    last = lax.axis_size("lat") - 1
    has_up = (lat > 0).astype(F32)
    has_down = (lat < last).astype(F32)
    even = lax.axis_index("comp") == 0
    first_col = lax.broadcasted_iota(jnp.int32, (COLS, WIDTH), 0) == 0
    final_col = lax.broadcasted_iota(jnp.int32, (COLS, WIDTH), 0) == COLS - 1

    def tap(i, j):
        return k_ref[block, i, j : j + 1, :]

    for m in range(2):
        rows = [
            up_ref[m].astype(F32) * has_up,
            top_ref[m].astype(F32),
            bot_ref[m].astype(F32),
            down_ref[m].astype(F32) * has_down,
        ]
        for r in range(2):
            a, b, c = rows[r : r + 3]
            mid = tap(0, 1) * a + (tap(1, 1) + 1.0) * b + tap(2, 1) * c
            west = tap(0, 0) * a + tap(1, 0) * b + tap(2, 0) * c
            east = tap(0, 2) * a + tap(1, 2) * b + tap(2, 2) * c
            right = west[COLS - 1 :, :]
            left = east[:1, :]
            i = 2 * m + r
            mate_ref[i : i + 1, :] = jnp.where(even, right, left)
            far_ref[i : i + 1, :] = jnp.where(even, left, right)
            part_ref[m, r] = (
                mid
                + jnp.where(first_col, 0.0, shift_cols(west, 1, 0))
                + jnp.where(final_col, 0.0, shift_cols(east, -1, 0))
            )


def conv_call(block, top, bot, up, down, kernels):
    shape = (2, 2, COLS, WIDTH)
    return pl.pallas_call(
        lambda *refs: conv_kernel(block, *refs),
        out_shape=(
            pltpu.VMEM(shape, F32),
            pltpu.VMEM((4, WIDTH), F32),
            pltpu.VMEM((4, WIDTH), F32),
        ),
        in_specs=[VM] * 5,
        out_specs=(VM,) * 3,
        compiler_params=PARAMS,
        name=f"conv_{block}",
    )(*near(top, bot, up, down, kernels))


def block_body(block, scale_ref, part_ref, mate_ref, far_ref, mask_ref, gain_ref, mlp_gain_ref,
               min_ref, mout_ref, weights, store):
    qkv_ref, out_ref, up_ref, down_ref = weights
    first_col = lax.broadcasted_iota(jnp.int32, (COLS, WIDTH), 0) == 0
    final_col = lax.broadcasted_iota(jnp.int32, (COLS, WIDTH), 0) == COLS - 1
    mean_matrix = head_mean(256)
    even = lax.axis_index("comp") == 0
    for m in range(2):
        rows = []
        for r in range(2):
            i = 2 * m + r
            x = part_ref[m, r]
            mate = mate_ref[i : i + 1, :]
            far = far_ref[i : i + 1, :]
            x = x + jnp.where(first_col, jnp.where(even, far, mate), 0.0)
            x = x + jnp.where(final_col, jnp.where(even, mate, far), 0.0)
            rows.append(x.astype(BF16))
        mixed = jnp.concatenate(rows, axis=0).astype(F32)
        normed = norm_rows(mixed, gain_ref[block : block + 1, :]).astype(BF16)
        qkv = dot(normed, qkv_ref())
        units = [unit(qkv[:, 256 * i : 256 * i + 256], mean_matrix) for i in range(3)]
        value = qkv[:, 2 * WIDTH :].astype(BF16)

        def lanes(j):
            return units[j // 2][:, 128 * (j % 2) : 128 * (j % 2) + 128]

        row_out = []
        for r in range(2):
            at = slice(COLS * r, COLS * r + COLS)
            pieces = []
            for j in range(3):
                pieces.append(
                    pair_attend(
                        lanes(j)[at],
                        lanes(3 + j)[at],
                        value[at, 128 * j : 128 * j + 128],
                        mask_ref[r],
                        scale_ref[block : block + 1, 2 * j : 2 * j + 1] * (LOG2E / 64),
                        scale_ref[block : block + 1, 2 * j + 1 : 2 * j + 2] * (LOG2E / 64),
                    )
                )
            row_out.append(jnp.concatenate(pieces, axis=1))
        attended = jnp.concatenate(row_out, axis=0)
        after = (mixed + dot(attended, out_ref())).astype(BF16)
        after_f = after.astype(F32)
        gain = mlp_gain_ref[block : block + 1, :] * min_ref[block, m : m + 1, :]
        scaled = norm_rows(after_f, gain).astype(BF16)
        total = after_f
        step = 512
        for h in range(0, HIDDEN, step):
            lifted = dot(scaled, up_ref(h, step)) * mout_ref[block, m : m + 1, h : h + step]
            total = total + dot(gelu(lifted).astype(BF16), down_ref(h, step))
        store(m, total.astype(BF16))


def weight_getters(block, refs):
    return (
        lambda: refs[0][block],
        lambda: refs[1][block],
        lambda h, n: refs[2][block, :, h : h + n],
        lambda h, n: refs[3][block, h : h + n, :],
    )


def first_kernel(scale_ref, part_ref, mate_ref, far_ref, mask_ref, gain_ref, mlp_gain_ref, min_ref,
                 mout_ref, qkv_h, out_h, up_h, down_h, top_ref, bot_ref):
    weights = weight_getters(0, (qkv_h, out_h, up_h, down_h))

    def store(m, value):
        top_ref[m] = value[:COLS]
        bot_ref[m] = value[COLS:]

    block_body(0, scale_ref, part_ref, mate_ref, far_ref, mask_ref, gain_ref, mlp_gain_ref,
               min_ref, mout_ref, weights, store)


def second_kernel(scale_ref, part_ref, mate_ref, far_ref, mask_ref, gain_ref, mlp_gain_ref, min_ref,
                  mout_ref, qkv_h, out_h, up_h, down_h, prev_ref, sea_ref, flux_ref,
                  cur_ref, start_ref):
    weights = weight_getters(1, (qkv_h, out_h, up_h, down_h))

    def store(m, value):
        flux = dot(value, flux_ref[...])
        for r in range(2):
            at = slice(COLS * r, COLS * r + COLS)
            cur_ref[m, r] = value[at]
            start = sea_ref[r] * (prev_ref[m, r].astype(F32) + flux[at])
            start_ref[:, 2 * m + r] = start.astype(BF16).reshape(16, 8, OCEAN)

    block_body(1, scale_ref, part_ref, mate_ref, far_ref, mask_ref, gain_ref, mlp_gain_ref,
               min_ref, mout_ref, weights, store)


def first_call(*args):
    row = pltpu.VMEM((2, COLS, WIDTH), BF16)
    return pl.pallas_call(
        first_kernel,
        out_shape=(row, row),
        in_specs=[VM] * 13,
        out_specs=(VM, VM),
        compiler_params=PARAMS,
        name="block_0",
    )(*near(*args))


def second_call(*args):
    return pl.pallas_call(
        second_kernel,
        out_shape=(
            pltpu.VMEM((2, 2, COLS, WIDTH), BF16),
            pltpu.VMEM((16, 4, 8, OCEAN), BF16),
        ),
        in_specs=[VM] * 16,
        out_specs=(VM, VM),
        compiler_params=PARAMS,
        name="block_1",
    )(*near(*args))


def taps3(field, k_ref, index):
    zero = jnp.zeros_like(field[:1])
    above = jnp.concatenate([zero, field[:-1]], axis=0)
    below = jnp.concatenate([field[1:], zero], axis=0)

    def column(j):
        return (
            k_ref[index, 0, j : j + 1, :] * above
            + k_ref[index, 1, j : j + 1, :] * field
            + k_ref[index, 2, j : j + 1, :] * below
        )

    return column(1) + shift_cols(column(0), 1, 1) + shift_cols(column(2), -1, 1)


def ocean_kernel(scale_ref, own_ref, west_ref, east_ref, k_ref, point_ref, gain_ref, qkv_ref,
                 out_ref, last_ref, pool_ref, wide_ref):
    mean_matrix = head_mean(128)
    row = lax.broadcasted_iota(jnp.int32, (128, 128), 0) % 8
    col = lax.broadcasted_iota(jnp.int32, (128, 128), 1) % 8
    mask = jnp.where(row == col, 1.0, 0.0)
    wide_ref[...] = jnp.zeros_like(wide_ref)
    for m in range(2):
        def rows_of(ref):
            even = ref[:, 2 * m].astype(F32)[:, None]
            odd = ref[:, 2 * m + 1].astype(F32)[:, None]
            return jnp.concatenate([even, odd], axis=1).reshape(32, 8, OCEAN)

        field = jnp.concatenate([rows_of(west_ref), rows_of(own_ref), rows_of(east_ref)], axis=1)
        act = taps3(field, k_ref, 0).astype(BF16).reshape(32 * 24, OCEAN)
        fine = gelu(dot(act, point_ref[0])).astype(BF16).astype(F32)
        fine4 = fine.reshape(16, 2, 24, OCEAN)
        pool_ref[...] = (fine4[:, 0] + fine4[:, 1]).reshape(16 * 24, OCEAN)
        coarse = []
        for i in range(16):
            coarse.append(
                pool_ref[pl.ds(24 * i + 4, 8, stride=2), :]
                + pool_ref[pl.ds(24 * i + 5, 8, stride=2), :]
            )
        coarse = (jnp.concatenate(coarse, axis=0) * 0.25).astype(BF16).astype(F32)
        act = taps3(coarse.reshape(16, 8, OCEAN), k_ref, 1).astype(BF16).reshape(128, OCEAN)
        first = gelu(dot(act, point_ref[1])).astype(BF16).astype(F32)
        normed = norm_rows(first, gain_ref[...]).astype(BF16)
        qkv = dot(normed, qkv_ref[...])
        attended = pair_attend(
            unit(qkv[:, :128], mean_matrix),
            unit(qkv[:, 128:256], mean_matrix),
            qkv[:, 256:].astype(BF16),
            mask,
            scale_ref[:, 0:1] * (LOG2E / 64),
            scale_ref[:, 1:2] * (LOG2E / 64),
        )
        following = (first + dot(attended, out_ref[...])).astype(BF16).astype(F32)
        for i in range(16):
            piece = following[8 * i : 8 * i + 8]
            wide_ref[pl.ds(24 * i + 4, 8, stride=2), :] = piece
            wide_ref[pl.ds(24 * i + 5, 8, stride=2), :] = piece
        spread = wide_ref[...].reshape(16, 1, 24, OCEAN)
        merged = (fine4 + spread).astype(BF16).astype(F32).reshape(32, 24, OCEAN)
        act = taps3(merged, k_ref, 2)[:, 8:16].astype(BF16).reshape(16, 2, 8, OCEAN)
        last_ref[:, 2 * m] = act[:, 0]
        last_ref[:, 2 * m + 1] = act[:, 1]


def ocean_call(*args):
    return pl.pallas_call(
        ocean_kernel,
        out_shape=pltpu.VMEM((16, 4, 8, OCEAN), BF16),
        in_specs=[VM] * 9,
        out_specs=VM,
        compiler_params=PARAMS,
        scratch_shapes=[pltpu.VMEM((16 * 24, OCEAN), F32), pltpu.VMEM((16 * 24, OCEAN), F32)],
        name="ocean",
    )(*near(*args))


def final_kernel(last_ref, start_ref, cur_ref, sea_ref, point_ref, return_ref, air_hbm, water_hbm,
                 air_ref, water_ref, sems):
    copies = []
    for m in range(2):
        for r in range(2):
            i = 2 * m + r
            act = last_ref[:, i].reshape(COLS, OCEAN)
            lifted = gelu(dot(act, point_ref[2]))
            sea = sea_ref[r]
            water = (sea * (start_ref[:, i].reshape(COLS, OCEAN).astype(F32) + lifted)).astype(BF16)
            water_ref[m, r] = water
            back = dot(water, return_ref[...])
            sea3 = jnp.concatenate([sea, sea, sea], axis=1)
            air_ref[m, r] = (cur_ref[m, r].astype(F32) + sea3 * back).astype(BF16)
            for k, (src, dst) in enumerate(((water_ref, water_hbm), (air_ref, air_hbm))):
                copies.append(pltpu.make_async_copy(src.at[m, r], dst.at[m, r], sems.at[2 * i + k]))
                copies[-1].start()
    for copy in copies:
        copy.wait()


def final_call(*args):
    return pl.pallas_call(
        final_kernel,
        out_shape=(
            jax.ShapeDtypeStruct((2, 2, COLS, WIDTH), BF16),
            jax.ShapeDtypeStruct((2, 2, COLS, OCEAN), BF16),
        ),
        in_specs=[VM] * 6,
        out_specs=(ANY, ANY),
        scratch_shapes=[
            pltpu.VMEM((2, 2, COLS, WIDTH), BF16),
            pltpu.VMEM((2, 2, COLS, OCEAN), BF16),
            pltpu.SemaphoreType.DMA((8,)),
        ],
        compiler_params=PARAMS,
        name="final",
    )(*near(*args))


LON = ("lon", "comp")


def ring(count, step):
    return [(i, (i + step) % count) for i in range(count)]


def group_ring(step):
    lats = lax.axis_size("lat")
    sectors = lax.axis_size("lon") * lax.axis_size("comp")
    total = lats * sectors
    pairs = []
    for g in range(total):
        t = (g + step) % total
        pairs.append(((g % lats) * sectors + g // lats, (t % lats) * sectors + t // lats))
    return pairs


def mix(block, top, bot, kernels):
    lats = lax.axis_size("lat")
    sectors = lax.axis_size("lon") * lax.axis_size("comp")
    up = lax.ppermute(bot, "lat", ring(lats, 1))
    down = lax.ppermute(top, "lat", ring(lats, -1))
    part, mate, far = conv_call(block, top, bot, up, down, kernels)
    mate = lax.ppermute(mate, LON, [(i, i ^ 1) for i in range(sectors)])
    far = lax.ppermute(far, LON, [(i, (i + 2 * (i % 2) - 1) % sectors) for i in range(sectors)])
    return part, mate, far


def load_kernel(count, *refs):
    ids_ref, land_ref = refs[:2]
    sources = refs[2 : 2 + count]
    mask_ref, sea_ref = refs[2 + count : 4 + count]
    targets = refs[4 + count : 4 + 2 * count]
    sems = refs[-1]
    copies = [
        pltpu.make_async_copy(src, dst, sems.at[i]) for i, (src, dst) in enumerate(zip(sources, targets))
    ]
    for copy in copies:
        copy.start()
    for r in range(2):
        ids = jnp.broadcast_to(ids_ref[r : r + 1, :].astype(F32), (COLS, COLS))
        mask_ref[r] = (ids == ids.T).astype(F32)
        sea_ref[r] = jnp.broadcast_to(land_ref[r : r + 1, :].astype(F32), (COLS, COLS)).T
    for copy in copies:
        copy.wait()


def load_call(ids, land, *arrays):
    count = len(arrays)
    return pl.pallas_call(
        lambda *refs: load_kernel(count, *refs),
        out_shape=[pltpu.VMEM((2, COLS, COLS), F32)] * 2
        + [pltpu.VMEM(a.shape, a.dtype) for a in arrays],
        in_specs=[VM] * 2 + [ANY] * count,
        out_specs=[VM] * (2 + count),
        scratch_shapes=[pltpu.SemaphoreType.DMA((count,))],
        compiler_params=PARAMS,
        name="load",
    )(ids, land, *(pltpu.with_memory_space_constraint(a, pltpu.HBM) for a in arrays))


def per_device(atm_state, ocean_prev, land_sea, window_ids, conv_atm, attn_gain, qkv_matrix,
               attn_scales, out_matrix, mlp_gain, member_in, member_out, up_matrix, down_matrix,
               flux_matrix, conv_ocean, point_matrix, ocean_gain, ocean_qkv, ocean_scale, ocean_out,
               seaside_return_matrix):
    (mask, sea, conv_atm, attn_scales, attn_gain, mlp_gain, member_in, member_out, qkv_matrix,
     out_matrix, up_matrix, down_matrix, ocean_prev, flux_matrix, conv_ocean, point_matrix, ocean_gain,
     ocean_qkv, ocean_scale, ocean_out, seaside_return_matrix) = load_call(
        window_ids, land_sea, conv_atm, attn_scales, attn_gain, mlp_gain, member_in, member_out,
        qkv_matrix, out_matrix, up_matrix, down_matrix, ocean_prev, flux_matrix, conv_ocean,
        point_matrix, ocean_gain[None, :], ocean_qkv, ocean_scale[None, :], ocean_out,
        seaside_return_matrix,
    )
    small = (attn_gain, mlp_gain, member_in, member_out)
    weights = (qkv_matrix, out_matrix, up_matrix, down_matrix)

    part, mate, far = mix(0, atm_state[:, 0], atm_state[:, 1], conv_atm)
    top, bot = first_call(attn_scales, part, mate, far, mask, *small, *weights)
    part, mate, far = mix(1, top, bot, conv_atm)
    current, start = second_call(
        attn_scales, part, mate, far, mask, *small, *weights, ocean_prev, sea, flux_matrix
    )
    own = lax.all_to_all(start, "lat", 0, 0)
    axes = ("lat",) + LON
    west = lax.ppermute(own, axes, group_ring(1))
    east = lax.ppermute(own, axes, group_ring(-1))
    last = ocean_call(ocean_scale, own, west, east, conv_ocean, point_matrix,
                      ocean_gain, ocean_qkv, ocean_out)
    last = lax.all_to_all(last, "lat", 0, 0)
    return final_call(last, start, current, sea, point_matrix, seaside_return_matrix)


def solution(mesh):
    field = P(None, "lat", LON, None)
    column = P("lat", LON)
    return jax.shard_map(
        per_device,
        mesh=mesh,
        in_specs=(field, field, column, column) + (P(),) * 18,
        out_specs=(field, field),
        check_vma=False,
    )
```

```python
import jax
import jax.numpy as jnp
from jax import lax
from jax.experimental import pallas as pl
from jax.experimental.pallas import tpu as pltpu
from jax.sharding import PartitionSpec as P

WIDTH = 384
HEADS = 6
HIDDEN = 1536
OCEAN = 128
BLOCKS = 2
COLS = 128
NORM_EPS = 1e-05
UNIT_EPS = 1e-06
LOG2E = 1.4426950408889634
STEP = 768
F32 = jnp.float32
BF16 = jnp.bfloat16
VM = pl.BlockSpec(memory_space=pltpu.VMEM)
SM = pl.BlockSpec(memory_space=pltpu.SMEM)
ANY = pl.BlockSpec(memory_space=pl.ANY)
PARAMS = pltpu.CompilerParams(vmem_limit_bytes=20 * 1024 * 1024)


def near(*arrays):
    return tuple(pltpu.with_memory_space_constraint(a, pltpu.VMEM) for a in arrays)


def dot(a, b):
    return jnp.dot(a, b, preferred_element_type=F32)


def dot_t(a, b):
    return lax.dot_general(a, b, (((1,), (1,)), ((), ())), preferred_element_type=F32)


def gelu(v):
    half = v * 0.5
    return half + half * lax.erf(v * 0.7071067811865476)


def norm_rows(x, gain):
    centred = x - jnp.mean(x, axis=-1, keepdims=True)
    spread = jnp.mean(centred * centred, axis=-1, keepdims=True)
    return centred * lax.rsqrt(spread + NORM_EPS) * gain


def head_mean(size):
    row = lax.broadcasted_iota(jnp.int32, (size, size), 0) // 64
    col = lax.broadcasted_iota(jnp.int32, (size, size), 1) // 64
    return jnp.where(row == col, 1.0 / 64.0, 0.0).astype(BF16)


def unit(p, mean_matrix):
    square = (p * p).astype(BF16)
    return (p * lax.rsqrt(dot(square, mean_matrix) + UNIT_EPS)).astype(BF16)


def pair_attend(q, k, v, mask, scale_even, scale_odd):
    low = lax.broadcasted_iota(jnp.int32, q.shape, 1) < 64
    zero = jnp.zeros_like(q)
    stacked = jnp.concatenate([jnp.where(low, q, zero), jnp.where(low, zero, q)], axis=0)
    scores = dot_t(stacked, k)
    rows = q.shape[0]
    even = jnp.exp2(scores[:rows] * scale_even) * mask
    odd = jnp.exp2(scores[rows:] * scale_odd) * mask
    terms = jnp.concatenate([even, odd], axis=0).astype(BF16)
    ext = jnp.concatenate([v, jnp.ones_like(v)], axis=1)
    sums = dot(terms, ext)
    number = jnp.where(low, sums[:rows, :128], sums[rows:, :128])
    denom = jnp.where(low, sums[:rows, 128:], sums[rows:, 128:])
    return (number / denom).astype(BF16)


def shift_cols(t, step, axis):
    return pltpu.roll(t, step % t.shape[axis], axis)


def conv_kernel(block, top_ref, bot_ref, up_ref, down_ref, k_ref, part_ref, mate_ref, far_ref):
    lat = lax.axis_index("lat")
    last = lax.axis_size("lat") - 1
    has_up = (lat > 0).astype(F32)
    has_down = (lat < last).astype(F32)
    even = lax.axis_index("comp") == 0
    first_col = lax.broadcasted_iota(jnp.int32, (COLS, WIDTH), 0) == 0
    final_col = lax.broadcasted_iota(jnp.int32, (COLS, WIDTH), 0) == COLS - 1

    def tap(i, j):
        return k_ref[block, i, j : j + 1, :]

    for m in range(2):
        rows = [
            up_ref[m].astype(F32) * has_up,
            top_ref[m].astype(F32),
            bot_ref[m].astype(F32),
            down_ref[m].astype(F32) * has_down,
        ]
        for r in range(2):
            a, b, c = rows[r : r + 3]
            mid = tap(0, 1) * a + (tap(1, 1) + 1.0) * b + tap(2, 1) * c
            west = tap(0, 0) * a + tap(1, 0) * b + tap(2, 0) * c
            east = tap(0, 2) * a + tap(1, 2) * b + tap(2, 2) * c
            right = west[COLS - 1 :, :]
            left = east[:1, :]
            i = 2 * m + r
            mate_ref[i : i + 1, :] = jnp.where(even, right, left)
            far_ref[i : i + 1, :] = jnp.where(even, left, right)
            part_ref[m, r] = (
                mid
                + jnp.where(first_col, 0.0, shift_cols(west, 1, 0))
                + jnp.where(final_col, 0.0, shift_cols(east, -1, 0))
            )


def conv_call(block, top, bot, up, down, kernels):
    shape = (2, 2, COLS, WIDTH)
    return pl.pallas_call(
        lambda *refs: conv_kernel(block, *refs),
        out_shape=(
            pltpu.VMEM(shape, F32),
            pltpu.VMEM((4, WIDTH), F32),
            pltpu.VMEM((4, WIDTH), F32),
        ),
        in_specs=[VM] * 5,
        out_specs=(VM,) * 3,
        compiler_params=PARAMS,
        name=f"conv_{block}",
    )(*near(top, bot, up, down, kernels))


def block_body(block, scale_ref, part_ref, mate_ref, far_ref, mask_ref, gain_ref, mlp_gain_ref,
               min_ref, mout_ref, weights, store):
    qkv_ref, out_ref, up_ref, down_ref = weights
    first_col = lax.broadcasted_iota(jnp.int32, (COLS, WIDTH), 0) == 0
    final_col = lax.broadcasted_iota(jnp.int32, (COLS, WIDTH), 0) == COLS - 1
    mean_matrix = head_mean(256)
    even = lax.axis_index("comp") == 0
    rows = []
    for m in range(2):
        for r in range(2):
            i = 2 * m + r
            x = part_ref[m, r]
            mate = mate_ref[i : i + 1, :]
            far = far_ref[i : i + 1, :]
            x = x + jnp.where(first_col, jnp.where(even, far, mate), 0.0)
            x = x + jnp.where(final_col, jnp.where(even, mate, far), 0.0)
            rows.append(x.astype(BF16))
    mixed = jnp.concatenate(rows, axis=0).astype(F32)
    normed = norm_rows(mixed, gain_ref[block : block + 1, :]).astype(BF16)
    qkv = dot(normed, qkv_ref())
    units = [unit(qkv[:, 256 * i : 256 * i + 256], mean_matrix) for i in range(3)]
    value = qkv[:, 2 * WIDTH :].astype(BF16)

    def lanes(j):
        return units[j // 2][:, 128 * (j % 2) : 128 * (j % 2) + 128]

    row_out = []
    for i in range(4):
        at = slice(COLS * i, COLS * i + COLS)
        pieces = []
        for j in range(3):
            pieces.append(
                pair_attend(
                    lanes(j)[at],
                    lanes(3 + j)[at],
                    value[at, 128 * j : 128 * j + 128],
                    mask_ref[i % 2],
                    scale_ref[block : block + 1, 2 * j : 2 * j + 1] * (LOG2E / 64),
                    scale_ref[block : block + 1, 2 * j + 1 : 2 * j + 2] * (LOG2E / 64),
                )
            )
        row_out.append(jnp.concatenate(pieces, axis=1))
    attended = jnp.concatenate(row_out, axis=0)
    after = (mixed + dot(attended, out_ref())).astype(BF16)
    after_f = after.astype(F32)
    scaled = norm_rows(after_f, mlp_gain_ref[block : block + 1, :])
    scaled = jnp.concatenate(
        [
            (scaled[: 2 * COLS] * min_ref[block, 0:1, :]).astype(BF16),
            (scaled[2 * COLS :] * min_ref[block, 1:2, :]).astype(BF16),
        ],
        axis=0,
    )
    total = after_f
    for h in range(0, HIDDEN, STEP):
        lifted = dot(scaled, up_ref(h, STEP))
        active = jnp.concatenate(
            [
                gelu(lifted[: 2 * COLS] * mout_ref[block, 0:1, h : h + STEP]).astype(BF16),
                gelu(lifted[2 * COLS :] * mout_ref[block, 1:2, h : h + STEP]).astype(BF16),
            ],
            axis=0,
        )
        total = total + dot(active, down_ref(h, STEP))
    store(total.astype(BF16))


def weight_getters(block, refs):
    return (
        lambda: refs[0][block],
        lambda: refs[1][block],
        lambda h, n: refs[2][block, :, h : h + n],
        lambda h, n: refs[3][block, h : h + n, :],
    )


def first_kernel(scale_ref, part_ref, mate_ref, far_ref, mask_ref, gain_ref, mlp_gain_ref, min_ref,
                 mout_ref, qkv_h, out_h, up_h, down_h, top_ref, bot_ref):
    weights = weight_getters(0, (qkv_h, out_h, up_h, down_h))

    def store(value):
        for m in range(2):
            top_ref[m] = value[2 * m * COLS : (2 * m + 1) * COLS]
            bot_ref[m] = value[(2 * m + 1) * COLS : (2 * m + 2) * COLS]

    block_body(0, scale_ref, part_ref, mate_ref, far_ref, mask_ref, gain_ref, mlp_gain_ref,
               min_ref, mout_ref, weights, store)


def turned(value, straight):
    back = jnp.concatenate([value[j : j + 1] for j in reversed(range(value.shape[0]))], axis=0)
    return jnp.where(straight, value, back)


def second_kernel(scale_ref, part_ref, mate_ref, far_ref, mask_ref, gain_ref, mlp_gain_ref, min_ref,
                  mout_ref, qkv_h, out_h, up_h, down_h, prev_ref, sea_ref, flux_ref,
                  cur_ref, start_ref):
    weights = weight_getters(1, (qkv_h, out_h, up_h, down_h))

    straight = lax.axis_index("comp") == 0

    def store(value):
        flux = dot(value, flux_ref[...])
        for i in range(4):
            m, r = i // 2, i % 2
            at = slice(COLS * i, COLS * i + COLS)
            cur_ref[m, r] = value[at]
            start = sea_ref[r] * (prev_ref[m, r].astype(F32) + flux[at])
            start_ref[:, i] = turned(start.reshape(16, 8, OCEAN), straight).astype(BF16)

    block_body(1, scale_ref, part_ref, mate_ref, far_ref, mask_ref, gain_ref, mlp_gain_ref,
               min_ref, mout_ref, weights, store)


def first_call(*args):
    row = pltpu.VMEM((2, COLS, WIDTH), BF16)
    return pl.pallas_call(
        first_kernel,
        out_shape=(row, row),
        in_specs=[VM] * 13,
        out_specs=(VM, VM),
        compiler_params=PARAMS,
        name="block_0",
    )(*near(*args))


def second_call(*args):
    return pl.pallas_call(
        second_kernel,
        out_shape=(
            pltpu.VMEM((2, 2, COLS, WIDTH), BF16),
            pltpu.VMEM((16, 4, 8, OCEAN), BF16),
        ),
        in_specs=[VM] * 16,
        out_specs=(VM, VM),
        compiler_params=PARAMS,
        name="block_1",
    )(*near(*args))


def taps3(field, k_ref, index):
    zero = jnp.zeros_like(field[:1])
    above = jnp.concatenate([zero, field[:-1]], axis=0)
    below = jnp.concatenate([field[1:], zero], axis=0)

    def column(j):
        return (
            k_ref[index, 0, j : j + 1, :] * above
            + k_ref[index, 1, j : j + 1, :] * field
            + k_ref[index, 2, j : j + 1, :] * below
        )

    return column(1) + shift_cols(column(0), 1, 1) + shift_cols(column(2), -1, 1)


def ocean_kernel(scale_ref, own_ref, pair_ref, next_ref, k_ref, point_ref, gain_ref, qkv_ref,
                 out_ref, last_ref, pool_ref, wide_ref):
    mean_matrix = head_mean(128)
    row = lax.broadcasted_iota(jnp.int32, (128, 128), 0) % 8
    col = lax.broadcasted_iota(jnp.int32, (128, 128), 1) % 8
    mask = jnp.where(row == col, 1.0, 0.0)
    wide_ref[...] = jnp.zeros_like(wide_ref)
    first_of_pair = (lax.axis_index("lat") + lax.axis_index("comp")) % 2 == 0
    for m in range(2):
        def rows_of(ref):
            even = ref[:, 2 * m].astype(F32)[:, None]
            odd = ref[:, 2 * m + 1].astype(F32)[:, None]
            return jnp.concatenate([even, odd], axis=1).reshape(32, 8, OCEAN)

        pair = rows_of(pair_ref)
        following = rows_of(next_ref)
        west = jnp.where(first_of_pair, following, pair)
        east = jnp.where(first_of_pair, pair, following)
        field = jnp.concatenate([west, rows_of(own_ref), east], axis=1)
        act = taps3(field, k_ref, 0).astype(BF16).reshape(32 * 24, OCEAN)
        fine = gelu(dot(act, point_ref[0])).astype(BF16).astype(F32)
        fine4 = fine.reshape(16, 2, 24, OCEAN)
        pool_ref[...] = (fine4[:, 0] + fine4[:, 1]).reshape(16 * 24, OCEAN)
        coarse = []
        for i in range(16):
            coarse.append(
                pool_ref[pl.ds(24 * i + 4, 8, stride=2), :]
                + pool_ref[pl.ds(24 * i + 5, 8, stride=2), :]
            )
        coarse = (jnp.concatenate(coarse, axis=0) * 0.25).astype(BF16).astype(F32)
        act = taps3(coarse.reshape(16, 8, OCEAN), k_ref, 1).astype(BF16).reshape(128, OCEAN)
        first = gelu(dot(act, point_ref[1])).astype(BF16).astype(F32)
        normed = norm_rows(first, gain_ref[...]).astype(BF16)
        qkv = dot(normed, qkv_ref[...])
        attended = pair_attend(
            unit(qkv[:, :128], mean_matrix),
            unit(qkv[:, 128:256], mean_matrix),
            qkv[:, 256:].astype(BF16),
            mask,
            scale_ref[:, 0:1] * (LOG2E / 64),
            scale_ref[:, 1:2] * (LOG2E / 64),
        )
        following = (first + dot(attended, out_ref[...])).astype(BF16).astype(F32)
        for i in range(16):
            piece = following[8 * i : 8 * i + 8]
            wide_ref[pl.ds(24 * i + 4, 8, stride=2), :] = piece
            wide_ref[pl.ds(24 * i + 5, 8, stride=2), :] = piece
        spread = wide_ref[...].reshape(16, 1, 24, OCEAN)
        merged = (fine4 + spread).astype(BF16).astype(F32).reshape(32, 24, OCEAN)
        act = taps3(merged, k_ref, 2)[:, 8:16].astype(BF16).reshape(16, 2, 8, OCEAN)
        last_ref[:, 2 * m] = act[:, 0]
        last_ref[:, 2 * m + 1] = act[:, 1]


def ocean_call(*args):
    return pl.pallas_call(
        ocean_kernel,
        out_shape=pltpu.VMEM((16, 4, 8, OCEAN), BF16),
        in_specs=[VM] * 9,
        out_specs=VM,
        compiler_params=PARAMS,
        scratch_shapes=[pltpu.VMEM((16 * 24, OCEAN), F32), pltpu.VMEM((16 * 24, OCEAN), F32)],
        name="ocean",
    )(*near(*args))


def final_kernel(last_ref, start_ref, cur_ref, sea_ref, point_ref, return_ref, air_hbm, water_hbm,
                 air_ref, water_ref, sems):
    copies = []
    straight = lax.axis_index("comp") == 0
    for m in range(2):
        for r in range(2):
            i = 2 * m + r
            act = turned(last_ref[:, i].astype(F32), straight).astype(BF16).reshape(COLS, OCEAN)
            start = turned(start_ref[:, i].astype(F32), straight).reshape(COLS, OCEAN)
            lifted = gelu(dot(act, point_ref[2]))
            sea = sea_ref[r]
            water = (sea * (start + lifted)).astype(BF16)
            water_ref[m, r] = water
            back = dot(water, return_ref[...])
            sea3 = jnp.concatenate([sea, sea, sea], axis=1)
            air_ref[m, r] = (cur_ref[m, r].astype(F32) + sea3 * back).astype(BF16)
            for k, (src, dst) in enumerate(((water_ref, water_hbm), (air_ref, air_hbm))):
                copies.append(pltpu.make_async_copy(src.at[m, r], dst.at[m, r], sems.at[2 * i + k]))
                copies[-1].start()
    for copy in copies:
        copy.wait()


def final_call(*args):
    return pl.pallas_call(
        final_kernel,
        out_shape=(
            jax.ShapeDtypeStruct((2, 2, COLS, WIDTH), BF16),
            jax.ShapeDtypeStruct((2, 2, COLS, OCEAN), BF16),
        ),
        in_specs=[VM] * 6,
        out_specs=(ANY, ANY),
        scratch_shapes=[
            pltpu.VMEM((2, 2, COLS, WIDTH), BF16),
            pltpu.VMEM((2, 2, COLS, OCEAN), BF16),
            pltpu.SemaphoreType.DMA((8,)),
        ],
        compiler_params=PARAMS,
        name="final",
    )(*near(*args))


LON = ("lon", "comp")


def ring(count, step):
    return [(i, (i + step) % count) for i in range(count)]


def group_swap(first):
    lats = lax.axis_size("lat")
    sectors = lax.axis_size("lon") * lax.axis_size("comp")
    total = lats * sectors

    def device(g):
        sector, place = g // lats, g % lats
        lat = place if sector % 2 == 0 else lats - 1 - place
        return lat * sectors + sector

    pairs = []
    for g in range(first, total, 2):
        a, b = device(g), device((g + 1) % total)
        pairs += [(a, b), (b, a)]
    return sorted(pairs)


def mix(block, top, bot, kernels):
    lats = lax.axis_size("lat")
    sectors = lax.axis_size("lon") * lax.axis_size("comp")
    up = lax.ppermute(bot, "lat", ring(lats, 1))
    down = lax.ppermute(top, "lat", ring(lats, -1))
    part, mate, far = conv_call(block, top, bot, up, down, kernels)
    mate = lax.ppermute(mate, LON, [(i, i ^ 1) for i in range(sectors)])
    far = lax.ppermute(far, LON, [(i, (i + 2 * (i % 2) - 1) % sectors) for i in range(sectors)])
    return part, mate, far


def load_kernel(count, *refs):
    sources = refs[: 2 + count]
    mask_ref, sea_ref = refs[2 + count : 4 + count]
    ids_ref, land_ref, sems = refs[-3:]
    targets = (ids_ref, land_ref) + tuple(refs[4 + count : 4 + 2 * count])
    copies = [
        pltpu.make_async_copy(src, dst, sems.at[i]) for i, (src, dst) in enumerate(zip(sources, targets))
    ]
    for copy in copies:
        copy.start()
    for copy in copies[:2]:
        copy.wait()
    for r in range(2):
        ids = jnp.broadcast_to(ids_ref[r : r + 1, :].astype(F32), (COLS, COLS))
        mask_ref[r] = (ids == ids.T).astype(F32)
        sea_ref[r] = jnp.broadcast_to(land_ref[r : r + 1, :].astype(F32), (COLS, COLS)).T
    for copy in copies[2:]:
        copy.wait()


def load_call(ids, land, *arrays):
    count = len(arrays)
    return pl.pallas_call(
        lambda *refs: load_kernel(count, *refs),
        out_shape=[pltpu.VMEM((2, COLS, COLS), F32)] * 2
        + [pltpu.VMEM(a.shape, a.dtype) for a in arrays],
        in_specs=[ANY] * (2 + count),
        out_specs=[VM] * (2 + count),
        scratch_shapes=[
            pltpu.VMEM((2, COLS), jnp.int32),
            pltpu.VMEM((2, COLS), jnp.int32),
            pltpu.SemaphoreType.DMA((2 + count,)),
        ],
        compiler_params=PARAMS,
        name="load",
    )(*(pltpu.with_memory_space_constraint(a, pltpu.HBM) for a in (ids, land) + arrays))


def per_device(atm_state, ocean_prev, land_sea, window_ids, conv_atm, attn_gain, qkv_matrix,
               attn_scales, out_matrix, mlp_gain, member_in, member_out, up_matrix, down_matrix,
               flux_matrix, conv_ocean, point_matrix, ocean_gain, ocean_qkv, ocean_scale, ocean_out,
               seaside_return_matrix):
    (mask, sea, conv_atm, attn_scales, attn_gain, mlp_gain, member_in, member_out, qkv_matrix,
     out_matrix, up_matrix, down_matrix, ocean_prev, flux_matrix, conv_ocean, point_matrix, ocean_gain,
     ocean_qkv, ocean_scale, ocean_out, seaside_return_matrix) = load_call(
        window_ids, land_sea, conv_atm, attn_scales, attn_gain, mlp_gain, member_in, member_out,
        qkv_matrix, out_matrix, up_matrix, down_matrix, ocean_prev, flux_matrix, conv_ocean,
        point_matrix, ocean_gain[None, :], ocean_qkv, ocean_scale[None, :], ocean_out,
        seaside_return_matrix,
    )
    small = (attn_gain, mlp_gain, member_in, member_out)
    weights = (qkv_matrix, out_matrix, up_matrix, down_matrix)

    part, mate, far = mix(0, atm_state[:, 0], atm_state[:, 1], conv_atm)
    top, bot = first_call(attn_scales, part, mate, far, mask, *small, *weights)
    part, mate, far = mix(1, top, bot, conv_atm)
    current, start = second_call(
        attn_scales, part, mate, far, mask, *small, *weights, ocean_prev, sea, flux_matrix
    )
    own = lax.all_to_all(start, "lat", 0, 0)
    axes = ("lat",) + LON
    pair = lax.ppermute(own, axes, group_swap(0))
    following = lax.ppermute(own, axes, group_swap(1))
    last = ocean_call(ocean_scale, own, pair, following, conv_ocean, point_matrix,
                      ocean_gain, ocean_qkv, ocean_out)
    last = lax.all_to_all(last, "lat", 0, 0)
    return final_call(last, start, current, sea, point_matrix, seaside_return_matrix)


def solution(mesh):
    field = P(None, "lat", LON, None)
    column = P("lat", LON)
    return jax.shard_map(
        per_device,
        mesh=mesh,
        in_specs=(field, field, column, column) + (P(),) * 18,
        out_specs=(field, field),
        check_vma=False,
    )
```

```python
import jax
import jax.numpy as jnp
from jax import lax
from jax.experimental import pallas as pl
from jax.experimental.pallas import tpu as pltpu
from jax.sharding import PartitionSpec as P


WIDTH = 384
HEADS = 6
HIDDEN = 1536
OCEAN = 128
COLS = 128
NORM_EPS = 1e-05
UNIT_EPS = 1e-06
LOG2E = 1.4426950408889634
STEP = 768
GROUP = 4
F32 = jnp.float32
BF16 = jnp.bfloat16
VM = pl.BlockSpec(memory_space=pltpu.VMEM)
SM = pl.BlockSpec(memory_space=pltpu.SMEM)
ANY = pl.BlockSpec(memory_space=pl.ANY)
PARAMS = pltpu.CompilerParams(vmem_limit_bytes=20 * 1024 * 1024)


def near(*arrays):
    return tuple(pltpu.with_memory_space_constraint(a, pltpu.VMEM) for a in arrays)


def dot(a, b):
    return jnp.dot(a, b, preferred_element_type=F32)


def dot_t(a, b):
    return lax.dot_general(a, b, (((1,), (1,)), ((), ())), preferred_element_type=F32)


def gelu(v):
    half = v * 0.5
    return half + half * lax.erf(v * 0.7071067811865476)


def norm_rows(x, gain):
    centred = x - jnp.mean(x, axis=-1, keepdims=True)
    spread = jnp.mean(centred * centred, axis=-1, keepdims=True)
    return centred * lax.rsqrt(spread + NORM_EPS) * gain


def head_mean(size):
    row = lax.broadcasted_iota(jnp.int32, (size, size), 0) // 64
    col = lax.broadcasted_iota(jnp.int32, (size, size), 1) // 64
    return jnp.where(row == col, 1.0 / 64.0, 0.0).astype(BF16)


def unit(p, mean_matrix):
    square = (p * p).astype(BF16)
    return (p * lax.rsqrt(dot(square, mean_matrix) + UNIT_EPS)).astype(BF16)


def pair_scores(q, k):
    low = lax.broadcasted_iota(jnp.int32, q.shape, 1) < 64
    zero = jnp.zeros_like(q)
    return dot_t(jnp.concatenate([jnp.where(low, q, zero), jnp.where(low, zero, q)], axis=0), k)


def pair_terms(scores, mask, scale_even, scale_odd):
    rows = scores.shape[0] // 2
    even = jnp.exp2(scores[:rows] * scale_even) * mask
    odd = jnp.exp2(scores[rows:] * scale_odd) * mask
    return jnp.concatenate([even, odd], axis=0).astype(BF16)


def pair_result(terms, v):
    rows = v.shape[0]
    low = lax.broadcasted_iota(jnp.int32, v.shape, 1) < 64
    sums = dot(terms, jnp.concatenate([v, jnp.ones_like(v)], axis=1))
    number = jnp.where(low, sums[:rows, :128], sums[rows:, :128])
    denom = jnp.where(low, sums[:rows, 128:], sums[rows:, 128:])
    return (number / denom).astype(BF16)


def pair_attend(q, k, v, mask, scale_even, scale_odd):
    return pair_result(pair_terms(pair_scores(q, k), mask, scale_even, scale_odd), v)


def shift_cols(t, step, axis):
    return pltpu.roll(t, step % t.shape[axis], axis)


def conv_kernel(block, top_ref, bot_ref, up_ref, down_ref, k_ref, part_ref, mate_ref, far_ref):
    lat = lax.axis_index("lat")
    last = lax.axis_size("lat") - 1
    has_up = (lat > 0).astype(F32)
    has_down = (lat < last).astype(F32)
    even = lax.axis_index("comp") == 0
    first_col = lax.broadcasted_iota(jnp.int32, (COLS, WIDTH), 0) == 0
    final_col = lax.broadcasted_iota(jnp.int32, (COLS, WIDTH), 0) == COLS - 1

    def tap(i, j):
        return k_ref[i, j, block : block + 1, :]

    for m in range(2):
        rows = [
            up_ref[m].astype(F32) * has_up,
            top_ref[m].astype(F32),
            bot_ref[m].astype(F32),
            down_ref[m].astype(F32) * has_down,
        ]
        for r in range(2):
            a, b, c = rows[r : r + 3]
            mid = tap(0, 1) * a + (tap(1, 1) + 1.0) * b + tap(2, 1) * c
            west = tap(0, 0) * a + tap(1, 0) * b + tap(2, 0) * c
            east = tap(0, 2) * a + tap(1, 2) * b + tap(2, 2) * c
            right = west[COLS - 1 :, :]
            left = east[:1, :]
            i = 2 * m + r
            mate_ref[i : i + 1, :] = jnp.where(even, right, left)
            far_ref[i : i + 1, :] = jnp.where(even, left, right)
            part_ref[m, r] = (
                mid
                + jnp.where(first_col, 0.0, shift_cols(west, 1, 0))
                + jnp.where(final_col, 0.0, shift_cols(east, -1, 0))
            )


def conv_call(block, top, bot, up, down, kernels):
    shape = (2, 2, COLS, WIDTH)
    return pl.pallas_call(
        lambda *refs: conv_kernel(block, *refs),
        out_shape=(
            pltpu.VMEM(shape, F32),
            pltpu.VMEM((4, WIDTH), F32),
            pltpu.VMEM((4, WIDTH), F32),
        ),
        in_specs=[VM] * 5,
        out_specs=(VM,) * 3,
        compiler_params=PARAMS,
    )(*near(top, bot, up, down, kernels))


def block_body(block, scale_ref, part_ref, mate_ref, far_ref, mask_ref, gain_ref, mlp_gain_ref,
               min_ref, mout_ref, weights, store):
    qkv_ref, out_ref, up_ref, down_ref = weights
    first_col = lax.broadcasted_iota(jnp.int32, (COLS, WIDTH), 0) == 0
    final_col = lax.broadcasted_iota(jnp.int32, (COLS, WIDTH), 0) == COLS - 1
    mean_matrix = head_mean(256)
    even = lax.axis_index("comp") == 0
    rows = []
    for m in range(2):
        for r in range(2):
            i = 2 * m + r
            x = part_ref[m, r]
            mate = mate_ref[i : i + 1, :]
            far = far_ref[i : i + 1, :]
            x = x + jnp.where(first_col, jnp.where(even, far, mate), 0.0)
            x = x + jnp.where(final_col, jnp.where(even, mate, far), 0.0)
            rows.append(x.astype(BF16))
    mixed = jnp.concatenate(rows, axis=0).astype(F32)
    normed = norm_rows(mixed, gain_ref[block : block + 1, :]).astype(BF16)
    qkv = dot(normed, qkv_ref())
    units = [unit(qkv[:, 256 * i : 256 * i + 256], mean_matrix) for i in range(3)]
    value = qkv[:, 2 * WIDTH :].astype(BF16)

    def lanes(j):
        return units[j // 2][:, 128 * (j % 2) : 128 * (j % 2) + 128]

    scales = [
        scale_ref[block : block + 1, h : h + 1] * (LOG2E / 64) for h in range(HEADS)
    ]
    row_out = []
    for first in range(0, 4, GROUP):
        cells = [(i, j) for i in range(first, first + GROUP) for j in range(3)]
        spans = {i: slice(COLS * i, COLS * i + COLS) for i in range(first, first + GROUP)}
        scores = [pair_scores(lanes(j)[spans[i]], lanes(3 + j)[spans[i]]) for i, j in cells]
        terms = [
            pair_terms(x, mask_ref[i % 2], scales[2 * j], scales[2 * j + 1])
            for x, (i, j) in zip(scores, cells)
        ]
        results = [
            pair_result(t, value[spans[i], 128 * j : 128 * j + 128])
            for t, (i, j) in zip(terms, cells)
        ]
        for i in range(GROUP):
            row_out.append(jnp.concatenate(results[3 * i : 3 * i + 3], axis=1))
    attended = jnp.concatenate(row_out, axis=0)
    after = (mixed + dot(attended, out_ref())).astype(BF16)
    after_f = after.astype(F32)
    scaled = norm_rows(after_f, mlp_gain_ref[block : block + 1, :])
    scaled = jnp.concatenate(
        [
            (scaled[: 2 * COLS] * min_ref[block, 0:1, :]).astype(BF16),
            (scaled[2 * COLS :] * min_ref[block, 1:2, :]).astype(BF16),
        ],
        axis=0,
    )
    total = after_f
    for h in range(0, HIDDEN, STEP):
        lifted = dot(scaled, up_ref(h, STEP))
        active = jnp.concatenate(
            [
                gelu(lifted[: 2 * COLS] * mout_ref[block, 0:1, h : h + STEP]).astype(BF16),
                gelu(lifted[2 * COLS :] * mout_ref[block, 1:2, h : h + STEP]).astype(BF16),
            ],
            axis=0,
        )
        total = total + dot(active, down_ref(h, STEP))
    store(total.astype(BF16))


def weight_getters(refs):
    return (
        lambda: refs[0][...],
        lambda: refs[1][...],
        lambda h, n: refs[2][:, h : h + n],
        lambda h, n: refs[3][h : h + n, :],
    )


def first_kernel(scale_ref, part_ref, mate_ref, far_ref, mask_ref, gain_ref, mlp_gain_ref, min_ref,
                 mout_ref, qkv_h, out_h, up_h, down_h, top_ref, bot_ref):
    weights = weight_getters((qkv_h, out_h, up_h, down_h))

    def store(value):
        for m in range(2):
            top_ref[m] = value[2 * m * COLS : (2 * m + 1) * COLS]
            bot_ref[m] = value[(2 * m + 1) * COLS : (2 * m + 2) * COLS]

    block_body(0, scale_ref, part_ref, mate_ref, far_ref, mask_ref, gain_ref, mlp_gain_ref,
               min_ref, mout_ref, weights, store)


def turned(value, straight):
    back = jnp.concatenate([value[j : j + 1] for j in reversed(range(value.shape[0]))], axis=0)
    return jnp.where(straight, value, back)


def second_kernel(scale_ref, part_ref, mate_ref, far_ref, mask_ref, gain_ref, mlp_gain_ref, min_ref,
                  mout_ref, qkv_h, out_h, up_h, down_h, prev_ref, sea_ref, flux_ref,
                  cur_ref, start_ref):
    weights = weight_getters((qkv_h, out_h, up_h, down_h))

    straight = lax.axis_index("comp") == 0

    def store(value):
        flux = dot(value, flux_ref[...])
        for i in range(4):
            m, r = i // 2, i % 2
            at = slice(COLS * i, COLS * i + COLS)
            cur_ref[m, r] = value[at]
            start = sea_ref[r] * (prev_ref[m, r].astype(F32) + flux[at])
            start_ref[:, i] = turned(start.reshape(16, 8, OCEAN), straight).astype(BF16)

    block_body(1, scale_ref, part_ref, mate_ref, far_ref, mask_ref, gain_ref, mlp_gain_ref,
               min_ref, mout_ref, weights, store)


def first_call(*args):
    row = pltpu.VMEM((2, COLS, WIDTH), BF16)
    return pl.pallas_call(
        first_kernel,
        out_shape=(row, row),
        in_specs=[VM] * 13,
        out_specs=(VM, VM),
        compiler_params=PARAMS,
        name="block_0",
    )(*near(*args))


def second_call(*args):
    return pl.pallas_call(
        second_kernel,
        out_shape=(
            pltpu.VMEM((2, 2, COLS, WIDTH), BF16),
            pltpu.VMEM((16, 4, 8, OCEAN), BF16),
        ),
        in_specs=[VM] * 16,
        out_specs=(VM, VM),
        compiler_params=PARAMS,
        name="block_1",
    )(*near(*args))


def taps3(field, k_ref, index):
    zero = jnp.zeros_like(field[:1])
    above = jnp.concatenate([zero, field[:-1]], axis=0)
    below = jnp.concatenate([field[1:], zero], axis=0)

    def column(j):
        return (
            k_ref[index, 0, j : j + 1, :] * above
            + k_ref[index, 1, j : j + 1, :] * field
            + k_ref[index, 2, j : j + 1, :] * below
        )

    return column(1) + shift_cols(column(0), 1, 1) + shift_cols(column(2), -1, 1)


def ocean_kernel(scale_ref, own_ref, pair_ref, next_ref, k_ref, point_ref, gain_ref, qkv_ref,
                 out_ref, last_ref, pool_ref, wide_ref):
    mean_matrix = head_mean(128)
    row = lax.broadcasted_iota(jnp.int32, (128, 128), 0) % 8
    col = lax.broadcasted_iota(jnp.int32, (128, 128), 1) % 8
    mask = jnp.where(row == col, 1.0, 0.0)
    wide_ref[...] = jnp.zeros_like(wide_ref)
    first_of_pair = (lax.axis_index("lat") + lax.axis_index("comp")) % 2 == 0
    for m in range(2):
        def rows_of(ref):
            even = ref[:, 2 * m].astype(F32)[:, None]
            odd = ref[:, 2 * m + 1].astype(F32)[:, None]
            return jnp.concatenate([even, odd], axis=1).reshape(32, 8, OCEAN)

        pair = rows_of(pair_ref)
        following = rows_of(next_ref)
        west = jnp.where(first_of_pair, following, pair)
        east = jnp.where(first_of_pair, pair, following)
        field = jnp.concatenate([west, rows_of(own_ref), east], axis=1)
        act = taps3(field, k_ref, 0).astype(BF16).reshape(32 * 24, OCEAN)
        fine = gelu(dot(act, point_ref[0])).astype(BF16).astype(F32)
        fine4 = fine.reshape(16, 2, 24, OCEAN)
        pool_ref[...] = (fine4[:, 0] + fine4[:, 1]).reshape(16 * 24, OCEAN)
        coarse = []
        for i in range(16):
            coarse.append(
                pool_ref[pl.ds(24 * i + 4, 8, stride=2), :]
                + pool_ref[pl.ds(24 * i + 5, 8, stride=2), :]
            )
        coarse = (jnp.concatenate(coarse, axis=0) * 0.25).astype(BF16).astype(F32)
        act = taps3(coarse.reshape(16, 8, OCEAN), k_ref, 1).astype(BF16).reshape(128, OCEAN)
        first = gelu(dot(act, point_ref[1])).astype(BF16).astype(F32)
        normed = norm_rows(first, gain_ref[...]).astype(BF16)
        qkv = dot(normed, qkv_ref[...])
        attended = pair_attend(
            unit(qkv[:, :128], mean_matrix),
            unit(qkv[:, 128:256], mean_matrix),
            qkv[:, 256:].astype(BF16),
            mask,
            scale_ref[:, 0:1] * (LOG2E / 64),
            scale_ref[:, 1:2] * (LOG2E / 64),
        )
        following = (first + dot(attended, out_ref[...])).astype(BF16).astype(F32)
        for i in range(16):
            piece = following[8 * i : 8 * i + 8]
            wide_ref[pl.ds(24 * i + 4, 8, stride=2), :] = piece
            wide_ref[pl.ds(24 * i + 5, 8, stride=2), :] = piece
        spread = wide_ref[...].reshape(16, 1, 24, OCEAN)
        merged = (fine4 + spread).astype(BF16).astype(F32).reshape(32, 24, OCEAN)
        act = taps3(merged, k_ref, 2)[:, 8:16].astype(BF16).reshape(16, 2, 8, OCEAN)
        last_ref[:, 2 * m] = act[:, 0]
        last_ref[:, 2 * m + 1] = act[:, 1]


def ocean_call(*args):
    return pl.pallas_call(
        ocean_kernel,
        out_shape=pltpu.VMEM((16, 4, 8, OCEAN), BF16),
        in_specs=[VM] * 9,
        out_specs=VM,
        compiler_params=PARAMS,
        scratch_shapes=[pltpu.VMEM((16 * 24, OCEAN), F32), pltpu.VMEM((16 * 24, OCEAN), F32)],
        name="ocean",
    )(*near(*args))


def final_kernel(last_ref, start_ref, cur_ref, sea_ref, point_ref, return_ref, air_hbm, water_hbm,
                 air_ref, water_ref, sems):
    copies = []
    straight = lax.axis_index("comp") == 0
    for m in range(2):
        for r in range(2):
            i = 2 * m + r
            act = turned(last_ref[:, i].astype(F32), straight).astype(BF16).reshape(COLS, OCEAN)
            start = turned(start_ref[:, i].astype(F32), straight).reshape(COLS, OCEAN)
            lifted = gelu(dot(act, point_ref[2]))
            sea = sea_ref[r]
            water = (sea * (start + lifted)).astype(BF16)
            water_ref[m, r] = water
            back = dot(water, return_ref[...])
            sea3 = jnp.concatenate([sea, sea, sea], axis=1)
            air_ref[m, r] = (cur_ref[m, r].astype(F32) + sea3 * back).astype(BF16)
            for k, (src, dst) in enumerate(((water_ref, water_hbm), (air_ref, air_hbm))):
                copies.append(pltpu.make_async_copy(src.at[m, r], dst.at[m, r], sems.at[2 * i + k]))
                copies[-1].start()
    for copy in copies:
        copy.wait()


def final_call(*args):
    return pl.pallas_call(
        final_kernel,
        out_shape=(
            jax.ShapeDtypeStruct((2, 2, COLS, WIDTH), BF16),
            jax.ShapeDtypeStruct((2, 2, COLS, OCEAN), BF16),
        ),
        in_specs=[VM] * 6,
        out_specs=(ANY, ANY),
        scratch_shapes=[
            pltpu.VMEM((2, 2, COLS, WIDTH), BF16),
            pltpu.VMEM((2, 2, COLS, OCEAN), BF16),
            pltpu.SemaphoreType.DMA((8,)),
        ],
        compiler_params=PARAMS,
        name="final",
    )(*near(*args))


LON = ("lon", "comp")


def ring(count, step):
    return [(i, (i + step) % count) for i in range(count)]


def group_swap(first):
    lats = lax.axis_size("lat")
    sectors = lax.axis_size("lon") * lax.axis_size("comp")
    total = lats * sectors

    def device(g):
        sector, place = g // lats, g % lats
        lat = place if sector % 2 == 0 else lats - 1 - place
        return lat * sectors + sector

    pairs = []
    for g in range(first, total, 2):
        a, b = device(g), device((g + 1) % total)
        pairs += [(a, b), (b, a)]
    return sorted(pairs)


def mix(block, top, bot, kernels):
    lats = lax.axis_size("lat")
    sectors = lax.axis_size("lon") * lax.axis_size("comp")
    up = lax.ppermute(bot, "lat", ring(lats, 1))
    down = lax.ppermute(top, "lat", ring(lats, -1))
    part, mate, far = conv_call(block, top, bot, up, down, kernels)
    far = lax.ppermute(far, LON, [(i, (i + 2 * (i % 2) - 1) % sectors) for i in range(sectors)])
    mate = lax.ppermute(mate, LON, [(i, i ^ 1) for i in range(sectors)])
    return part, mate, far


def start_copies(sources, targets, sems):
    copies = [
        pltpu.make_async_copy(src, dst, sems.at[i]) for i, (src, dst) in enumerate(zip(sources, targets))
    ]
    for copy in copies:
        copy.start()
    return copies


def load_kernel(block, count, *refs):
    sources = [
        ref if i < count - 4 else ref.at[block] for i, ref in enumerate(refs[:count])
    ]
    if block == 0:
        mask_ref, sea_ref = refs[count : count + 2]
        ids_ref, land_ref, sems = refs[-3:]
        targets = (ids_ref, land_ref) + tuple(refs[count + 2 : -3])
        copies = start_copies(sources, targets, sems)
        for copy in copies[:2]:
            copy.wait()
        for r in range(2):
            ids = jnp.broadcast_to(ids_ref[r : r + 1, :].astype(F32), (COLS, COLS))
            mask_ref[r] = (ids == ids.T).astype(F32)
            sea_ref[r] = jnp.broadcast_to(land_ref[r : r + 1, :].astype(F32), (COLS, COLS)).T
        copies = copies[2:]
    else:
        copies = start_copies(sources, refs[count:-1], refs[-1])
    for copy in copies:
        copy.wait()


def load_call(block, *arrays):
    count = len(arrays)
    shapes = [a.shape for a in arrays[:-4]] + [a.shape[1:] for a in arrays[-4:]]
    outs = [pltpu.VMEM(s, a.dtype) for s, a in zip(shapes, arrays)]
    scratch = [pltpu.SemaphoreType.DMA((count,))]
    if block == 0:
        outs = [pltpu.VMEM((2, COLS, COLS), F32)] * 2 + outs[2:]
        scratch = [pltpu.VMEM((2, COLS), jnp.int32), pltpu.VMEM((2, COLS), jnp.int32)] + scratch
    return pl.pallas_call(
        lambda *refs: load_kernel(block, count, *refs),
        out_shape=outs,
        in_specs=[ANY] * count,
        out_specs=[VM] * len(outs),
        scratch_shapes=scratch,
        compiler_params=PARAMS,
    )(*(pltpu.with_memory_space_constraint(a, pltpu.HBM) for a in arrays))


def per_device(atm_state, ocean_prev, land_sea, window_ids, conv_atm, attn_gain, qkv_matrix,
               attn_scales, out_matrix, mlp_gain, member_in, member_out, up_matrix, down_matrix,
               flux_matrix, conv_ocean, point_matrix, ocean_gain, ocean_qkv, ocean_scale, ocean_out,
               seaside_return_matrix):
    big = (qkv_matrix, out_matrix, up_matrix, down_matrix)
    mask, sea, conv_atm, attn_scales, attn_gain, mlp_gain, member_in, member_out, *weights = load_call(
        0, window_ids, land_sea, jnp.transpose(conv_atm, (1, 2, 0, 3)), attn_scales, attn_gain,
        mlp_gain, member_in, member_out, *big
    )
    small = (attn_gain, mlp_gain, member_in, member_out)
    part, mate, far = mix(0, atm_state[:, 0], atm_state[:, 1], conv_atm)
    top, bot = first_call(attn_scales, part, mate, far, mask, *small, *weights)

    (ocean_prev, flux_matrix, conv_ocean, point_matrix, ocean_gain, ocean_qkv, ocean_scale, ocean_out,
     seaside_return_matrix, *weights) = load_call(
        1, ocean_prev, flux_matrix, conv_ocean, point_matrix, ocean_gain[None, :], ocean_qkv,
        ocean_scale[None, :], ocean_out, seaside_return_matrix, *big
    )
    part, mate, far = mix(1, top, bot, conv_atm)
    current, start = second_call(
        attn_scales, part, mate, far, mask, *small, *weights, ocean_prev, sea, flux_matrix
    )
    own = lax.all_to_all(start, "lat", 0, 0)
    axes = ("lat",) + LON
    pair = lax.ppermute(own, axes, group_swap(0))
    following = lax.ppermute(own, axes, group_swap(1))
    last = ocean_call(ocean_scale, own, pair, following, conv_ocean, point_matrix,
                      ocean_gain, ocean_qkv, ocean_out)
    last = lax.all_to_all(last, "lat", 0, 0)
    return final_call(last, start, current, sea, point_matrix, seaside_return_matrix)


def solution(mesh):
    field = P(None, "lat", LON, None)
    column = P("lat", LON)
    return jax.shard_map(
        per_device,
        mesh=mesh,
        in_specs=(field, field, column, column) + (P(),) * 18,
        out_specs=(field, field),
        check_vma=False,
    )
```

```python
import jax
import jax.numpy as jnp
from jax import lax
from jax.experimental import pallas as pl
from jax.experimental.pallas import tpu as pltpu
from jax.sharding import PartitionSpec as P


WIDTH = 384
HEADS = 6
HIDDEN = 1536
OCEAN = 128
COLS = 128
NORM_EPS = 1e-05
UNIT_EPS = 1e-06
LOG2E = 1.4426950408889634
STEP = 768
GROUP = 4
F32 = jnp.float32
BF16 = jnp.bfloat16
VM = pl.BlockSpec(memory_space=pltpu.VMEM)
SM = pl.BlockSpec(memory_space=pltpu.SMEM)
ANY = pl.BlockSpec(memory_space=pl.ANY)
PARAMS = pltpu.CompilerParams(vmem_limit_bytes=20 * 1024 * 1024)


def near(*arrays):
    return tuple(pltpu.with_memory_space_constraint(a, pltpu.VMEM) for a in arrays)


def dot(a, b):
    return jnp.dot(a, b, preferred_element_type=F32)


def dot_t(a, b):
    return lax.dot_general(a, b, (((1,), (1,)), ((), ())), preferred_element_type=F32)


def gelu(v):
    half = v * 0.5
    return half + half * lax.erf(v * 0.7071067811865476)


def norm_rows(x, gain):
    centred = x - jnp.mean(x, axis=-1, keepdims=True)
    spread = jnp.mean(centred * centred, axis=-1, keepdims=True)
    return centred * lax.rsqrt(spread + NORM_EPS) * gain


def head_mean(size):
    row = lax.broadcasted_iota(jnp.int32, (size, size), 0) // 64
    col = lax.broadcasted_iota(jnp.int32, (size, size), 1) // 64
    return jnp.where(row == col, 1.0 / 64.0, 0.0).astype(BF16)


def unit(p, mean_matrix):
    square = (p * p).astype(BF16)
    return (p * lax.rsqrt(dot(square, mean_matrix) + UNIT_EPS)).astype(BF16)


def pair_scores(q, k):
    low = lax.broadcasted_iota(jnp.int32, q.shape, 1) < 64
    zero = jnp.zeros_like(q)
    return dot_t(jnp.concatenate([jnp.where(low, q, zero), jnp.where(low, zero, q)], axis=0), k)


def pair_terms(scores, mask, scale_even, scale_odd):
    rows = scores.shape[0] // 2
    even = jnp.exp2(scores[:rows] * scale_even) * mask
    odd = jnp.exp2(scores[rows:] * scale_odd) * mask
    return jnp.concatenate([even, odd], axis=0).astype(BF16)


def pair_result(terms, v):
    rows = v.shape[0]
    low = lax.broadcasted_iota(jnp.int32, v.shape, 1) < 64
    sums = dot(terms, jnp.concatenate([v, jnp.ones_like(v)], axis=1))
    number = jnp.where(low, sums[:rows, :128], sums[rows:, :128])
    denom = jnp.where(low, sums[:rows, 128:], sums[rows:, 128:])
    return (number / denom).astype(BF16)


def pair_attend(q, k, v, mask, scale_even, scale_odd):
    return pair_result(pair_terms(pair_scores(q, k), mask, scale_even, scale_odd), v)


def shift_cols(t, step, axis):
    return pltpu.roll(t, step % t.shape[axis], axis)


def edge_kernel(block, top_ref, bot_ref, up_ref, down_ref, k_ref, *refs):
    mate_ref, far_ref = refs[-2:]
    has_up, has_down = inner_rows()
    even = lax.axis_index("comp") == 0

    def tap(i, j):
        return k_ref[i, j, block : block + 1, :]

    for m in range(2):
        def column(c):
            return [
                up_ref[m, c : c + 1, :].astype(F32) * has_up,
                top_ref[m, c : c + 1, :].astype(F32),
                bot_ref[m, c : c + 1, :].astype(F32),
                down_ref[m, c : c + 1, :].astype(F32) * has_down,
            ]

        final, first = column(COLS - 1), column(0)
        for r in range(2):
            right = sum(tap(i, 0) * final[r + i] for i in range(3))
            left = sum(tap(i, 2) * first[r + i] for i in range(3))
            i = 2 * m + r
            mate_ref[i : i + 1, :] = jnp.where(even, right, left)
            far_ref[i : i + 1, :] = jnp.where(even, left, right)


def inner_rows():
    lat = lax.axis_index("lat")
    return (lat > 0).astype(F32), (lat < lax.axis_size("lat") - 1).astype(F32)


def conv_kernel(block, top_ref, bot_ref, up_ref, down_ref, k_ref, part_ref):
    has_up, has_down = inner_rows()
    first_col = lax.broadcasted_iota(jnp.int32, (COLS, WIDTH), 0) == 0
    final_col = lax.broadcasted_iota(jnp.int32, (COLS, WIDTH), 0) == COLS - 1

    def tap(i, j):
        return k_ref[i, j, block : block + 1, :]

    for m in range(2):
        rows = [
            up_ref[m].astype(F32) * has_up,
            top_ref[m].astype(F32),
            bot_ref[m].astype(F32),
            down_ref[m].astype(F32) * has_down,
        ]
        for r in range(2):
            a, b, c = rows[r : r + 3]
            mid = tap(0, 1) * a + (tap(1, 1) + 1.0) * b + tap(2, 1) * c
            west = tap(0, 0) * a + tap(1, 0) * b + tap(2, 0) * c
            east = tap(0, 2) * a + tap(1, 2) * b + tap(2, 2) * c
            part_ref[m, r] = (
                mid
                + jnp.where(first_col, 0.0, shift_cols(west, 1, 0))
                + jnp.where(final_col, 0.0, shift_cols(east, -1, 0))
            )


def edge_call(block, *args):
    return pl.pallas_call(
        lambda *refs: edge_kernel(block, *refs),
        out_shape=(pltpu.VMEM((4, WIDTH), F32), pltpu.VMEM((4, WIDTH), F32)),
        in_specs=[VM] * len(args),
        out_specs=(VM, VM),
        compiler_params=PARAMS,
    )(*near(*args))


def conv_call(block, *args):
    return pl.pallas_call(
        lambda *refs: conv_kernel(block, *refs),
        out_shape=pltpu.VMEM((2, 2, COLS, WIDTH), F32),
        in_specs=[VM] * 5,
        out_specs=VM,
        compiler_params=PARAMS,
    )(*near(*args))


def block_body(block, scale_ref, part_ref, mate_ref, far_ref, mask_ref, gain_ref, mlp_gain_ref,
               min_ref, mout_ref, weights, store):
    qkv_ref, out_ref, up_ref, down_ref = weights
    first_col = lax.broadcasted_iota(jnp.int32, (COLS, WIDTH), 0) == 0
    final_col = lax.broadcasted_iota(jnp.int32, (COLS, WIDTH), 0) == COLS - 1
    mean_matrix = head_mean(256)
    even = lax.axis_index("comp") == 0
    rows = []
    for m in range(2):
        for r in range(2):
            i = 2 * m + r
            x = part_ref[m, r]
            mate = mate_ref[i : i + 1, :]
            far = far_ref[i : i + 1, :]
            x = x + jnp.where(first_col, jnp.where(even, far, mate), 0.0)
            x = x + jnp.where(final_col, jnp.where(even, mate, far), 0.0)
            rows.append(x.astype(BF16))
    mixed = jnp.concatenate(rows, axis=0).astype(F32)
    normed = norm_rows(mixed, gain_ref[block : block + 1, :]).astype(BF16)
    qkv = dot(normed, qkv_ref())
    units = [unit(qkv[:, 256 * i : 256 * i + 256], mean_matrix) for i in range(3)]
    value = qkv[:, 2 * WIDTH :].astype(BF16)

    def lanes(j):
        return units[j // 2][:, 128 * (j % 2) : 128 * (j % 2) + 128]

    scales = [
        scale_ref[block : block + 1, h : h + 1] * (LOG2E / 64) for h in range(HEADS)
    ]
    row_out = []
    for first in range(0, 4, GROUP):
        cells = [(i, j) for i in range(first, first + GROUP) for j in range(3)]
        spans = {i: slice(COLS * i, COLS * i + COLS) for i in range(first, first + GROUP)}
        scores = [pair_scores(lanes(j)[spans[i]], lanes(3 + j)[spans[i]]) for i, j in cells]
        terms = [
            pair_terms(x, mask_ref[i % 2], scales[2 * j], scales[2 * j + 1])
            for x, (i, j) in zip(scores, cells)
        ]
        results = [
            pair_result(t, value[spans[i], 128 * j : 128 * j + 128])
            for t, (i, j) in zip(terms, cells)
        ]
        for i in range(GROUP):
            row_out.append(jnp.concatenate(results[3 * i : 3 * i + 3], axis=1))
    attended = jnp.concatenate(row_out, axis=0)
    after = (mixed + dot(attended, out_ref())).astype(BF16)
    after_f = after.astype(F32)
    scaled = norm_rows(after_f, mlp_gain_ref[block : block + 1, :])
    scaled = jnp.concatenate(
        [
            (scaled[: 2 * COLS] * min_ref[block, 0:1, :]).astype(BF16),
            (scaled[2 * COLS :] * min_ref[block, 1:2, :]).astype(BF16),
        ],
        axis=0,
    )
    total = after_f
    for h in range(0, HIDDEN, STEP):
        lifted = dot(scaled, up_ref(h, STEP))
        active = jnp.concatenate(
            [
                gelu(lifted[: 2 * COLS] * mout_ref[block, 0:1, h : h + STEP]).astype(BF16),
                gelu(lifted[2 * COLS :] * mout_ref[block, 1:2, h : h + STEP]).astype(BF16),
            ],
            axis=0,
        )
        total = total + dot(active, down_ref(h, STEP))
    store(total.astype(BF16))


def weight_getters(refs):
    return (
        lambda: refs[0][...],
        lambda: refs[1][...],
        lambda h, n: refs[2][:, h : h + n],
        lambda h, n: refs[3][h : h + n, :],
    )


def first_kernel(scale_ref, part_ref, mate_ref, far_ref, mask_ref, gain_ref, mlp_gain_ref, min_ref,
                 mout_ref, qkv_h, out_h, up_h, down_h, top_ref, bot_ref):
    weights = weight_getters((qkv_h, out_h, up_h, down_h))

    def store(value):
        for m in range(2):
            top_ref[m] = value[2 * m * COLS : (2 * m + 1) * COLS]
            bot_ref[m] = value[(2 * m + 1) * COLS : (2 * m + 2) * COLS]

    block_body(0, scale_ref, part_ref, mate_ref, far_ref, mask_ref, gain_ref, mlp_gain_ref,
               min_ref, mout_ref, weights, store)


def turned(value, straight):
    back = jnp.concatenate([value[j : j + 1] for j in reversed(range(value.shape[0]))], axis=0)
    return jnp.where(straight, value, back)


def second_kernel(scale_ref, part_ref, mate_ref, far_ref, mask_ref, gain_ref, mlp_gain_ref, min_ref,
                  mout_ref, qkv_h, out_h, up_h, down_h, prev_ref, sea_ref, flux_ref,
                  cur_ref, start_ref):
    weights = weight_getters((qkv_h, out_h, up_h, down_h))

    straight = lax.axis_index("comp") == 0

    def store(value):
        flux = dot(value, flux_ref[...])
        for i in range(4):
            m, r = i // 2, i % 2
            at = slice(COLS * i, COLS * i + COLS)
            cur_ref[m, r] = value[at]
            start = sea_ref[r] * (prev_ref[m, r].astype(F32) + flux[at])
            start_ref[:, i] = turned(start.reshape(16, 8, OCEAN), straight).astype(BF16)

    block_body(1, scale_ref, part_ref, mate_ref, far_ref, mask_ref, gain_ref, mlp_gain_ref,
               min_ref, mout_ref, weights, store)


def first_call(*args):
    row = pltpu.VMEM((2, COLS, WIDTH), BF16)
    return pl.pallas_call(
        first_kernel,
        out_shape=(row, row),
        in_specs=[VM] * 13,
        out_specs=(VM, VM),
        compiler_params=PARAMS,
        name="block_0",
    )(*near(*args))


def second_call(*args):
    return pl.pallas_call(
        second_kernel,
        out_shape=(
            pltpu.VMEM((2, 2, COLS, WIDTH), BF16),
            pltpu.VMEM((16, 4, 8, OCEAN), BF16),
        ),
        in_specs=[VM] * 16,
        out_specs=(VM, VM),
        compiler_params=PARAMS,
        name="block_1",
    )(*near(*args))


def taps3(columns, k_ref, index):
    total = 0.0
    for j, field in enumerate(columns):
        zero = jnp.zeros_like(field[:1])
        above = jnp.concatenate([zero, field[:-1]], axis=0)
        below = jnp.concatenate([field[1:], zero], axis=0)
        total = total + (
            k_ref[index, 0, j : j + 1, :] * above
            + k_ref[index, 1, j : j + 1, :] * field
            + k_ref[index, 2, j : j + 1, :] * below
        )
    return total


def ocean_kernel(scale_ref, own_ref, pair_ref, next_ref, k_ref, point_ref, gain_ref, qkv_ref,
                 out_ref, last_ref, field_ref, pool_ref, wide_ref, merged_ref):
    mean_matrix = head_mean(128)
    row = lax.broadcasted_iota(jnp.int32, (128, 128), 0) % 8
    col = lax.broadcasted_iota(jnp.int32, (128, 128), 1) % 8
    mask = jnp.where(row == col, 1.0, 0.0)
    first_of_pair = (lax.axis_index("lat") + lax.axis_index("comp")) % 2 == 0
    fine_all = []
    for m in range(2):
        def rows_of(ref):
            even = ref[:, 2 * m].astype(F32)[:, None]
            odd = ref[:, 2 * m + 1].astype(F32)[:, None]
            return jnp.concatenate([even, odd], axis=1).reshape(32, 8, OCEAN)

        pair = rows_of(pair_ref)
        following = rows_of(next_ref)
        field_ref[m, :, 0:8, :] = jnp.where(first_of_pair, following, pair)
        field_ref[m, :, 8:16, :] = rows_of(own_ref)
        field_ref[m, :, 16:24, :] = jnp.where(first_of_pair, pair, following)
        act = taps3([field_ref[m, :, 3 + j : 19 + j, :] for j in range(3)], k_ref, 0)
        act = act.astype(BF16).reshape(32 * 16, OCEAN)
        fine = gelu(dot(act, point_ref[0])).astype(BF16).astype(F32).reshape(16, 2, 16, OCEAN)
        fine_all.append(fine)
        pool_ref[m] = (fine[:, 0] + fine[:, 1]).reshape(256, OCEAN)
    coarse = []
    for m in range(2):
        pooled = pool_ref[m, pl.ds(0, 128, stride=2), :] + pool_ref[m, pl.ds(1, 128, stride=2), :]
        coarse.append((pooled * 0.25).astype(BF16).astype(F32).reshape(16, 8, OCEAN))
    acts = []
    for m in range(2):
        columns = (shift_cols(coarse[m], 1, 1), coarse[m], shift_cols(coarse[m], -1, 1))
        acts.append(taps3(columns, k_ref, 1).astype(BF16).reshape(128, OCEAN))
    first = gelu(dot(jnp.concatenate(acts, axis=0), point_ref[1])).astype(BF16).astype(F32)
    normed = norm_rows(first, gain_ref[...]).astype(BF16)
    qkv = dot(normed, qkv_ref[...])
    query = unit(qkv[:, :128], mean_matrix)
    key = unit(qkv[:, 128:256], mean_matrix)
    value = qkv[:, 256:].astype(BF16)
    attended = []
    for m in range(2):
        at = slice(128 * m, 128 * m + 128)
        attended.append(
            pair_attend(
                query[at],
                key[at],
                value[at],
                mask,
                scale_ref[:, 0:1] * (LOG2E / 64),
                scale_ref[:, 1:2] * (LOG2E / 64),
            )
        )
    attended = jnp.concatenate(attended, axis=0)
    coarse_next = (first + dot(attended, out_ref[...])).astype(BF16).astype(F32)
    for m in range(2):
        piece = coarse_next[128 * m : 128 * m + 128]
        wide_ref[m, pl.ds(0, 128, stride=2), :] = piece
        wide_ref[m, pl.ds(1, 128, stride=2), :] = piece
    for m in range(2):
        spread = wide_ref[m].reshape(16, 1, 16, OCEAN)
        merged_ref[m] = (fine_all[m] + spread).astype(BF16).astype(F32).reshape(32, 16, OCEAN)
        act = taps3([merged_ref[m, :, 3 + j : 11 + j, :] for j in range(3)], k_ref, 2)
        act = act.astype(BF16).reshape(16, 2, 8, OCEAN)
        last_ref[:, 2 * m] = act[:, 0]
        last_ref[:, 2 * m + 1] = act[:, 1]


def ocean_call(*args):
    return pl.pallas_call(
        ocean_kernel,
        out_shape=pltpu.VMEM((16, 4, 8, OCEAN), BF16),
        in_specs=[VM] * 9,
        out_specs=VM,
        compiler_params=PARAMS,
        scratch_shapes=[
            pltpu.VMEM((2, 32, 24, OCEAN), F32),
            pltpu.VMEM((2, 256, OCEAN), F32),
            pltpu.VMEM((2, 256, OCEAN), F32),
            pltpu.VMEM((2, 32, 16, OCEAN), F32),
        ],
        name="ocean",
    )(*near(*args))


def final_kernel(last_ref, start_ref, cur_ref, sea_ref, point_ref, return_ref, air_hbm, water_hbm,
                 air_ref, water_ref, sems):
    copies = []

    def send(src, dst, m, r, k):
        copies.append(pltpu.make_async_copy(src.at[m, r], dst.at[m, r], sems.at[k]))
        copies[-1].start()

    straight = lax.axis_index("comp") == 0
    acts = [
        turned(last_ref[:, i].astype(F32), straight).astype(BF16).reshape(COLS, OCEAN) for i in range(4)
    ]
    lifted = gelu(dot(jnp.concatenate(acts, axis=0), point_ref[2]))
    waters = []
    for i in range(4):
        m, r = i // 2, i % 2
        start = turned(start_ref[:, i].astype(F32), straight).reshape(COLS, OCEAN)
        waters.append((sea_ref[r] * (start + lifted[COLS * i : COLS * i + COLS])).astype(BF16))
        water_ref[m, r] = waters[i]
        send(water_ref, water_hbm, m, r, i)
    back = dot(jnp.concatenate(waters, axis=0), return_ref[...])
    for i in range(4):
        m, r = i // 2, i % 2
        sea = jnp.concatenate([sea_ref[r]] * 3, axis=1)
        air_ref[m, r] = (cur_ref[m, r].astype(F32) + sea * back[COLS * i : COLS * i + COLS]).astype(BF16)
        send(air_ref, air_hbm, m, r, 4 + i)
    for copy in copies:
        copy.wait()


def final_call(*args):
    return pl.pallas_call(
        final_kernel,
        out_shape=(
            jax.ShapeDtypeStruct((2, 2, COLS, WIDTH), BF16),
            jax.ShapeDtypeStruct((2, 2, COLS, OCEAN), BF16),
        ),
        in_specs=[VM] * 6,
        out_specs=(ANY, ANY),
        scratch_shapes=[
            pltpu.VMEM((2, 2, COLS, WIDTH), BF16),
            pltpu.VMEM((2, 2, COLS, OCEAN), BF16),
            pltpu.SemaphoreType.DMA((8,)),
        ],
        compiler_params=PARAMS,
        name="final",
    )(*near(*args))


LON = ("lon", "comp")


def ring(count, step):
    return [(i, (i + step) % count) for i in range(count)]


def group_swap(first):
    lats = lax.axis_size("lat")
    sectors = lax.axis_size("lon") * lax.axis_size("comp")
    total = lats * sectors

    def device(g):
        sector, place = g // lats, g % lats
        lat = place if sector % 2 == 0 else lats - 1 - place
        return lat * sectors + sector

    pairs = []
    for g in range(first, total, 2):
        a, b = device(g), device((g + 1) % total)
        pairs += [(a, b), (b, a)]
    return sorted(pairs)


def mix(block, top, bot, kernels, *after):
    lats = lax.axis_size("lat")
    sectors = lax.axis_size("lon") * lax.axis_size("comp")
    up = lax.ppermute(bot, "lat", ring(lats, 1))
    down = lax.ppermute(top, "lat", ring(lats, -1))
    mate, far = edge_call(block, top, bot, up, down, kernels, *after)
    far = lax.ppermute(far, LON, [(i, (i + 2 * (i % 2) - 1) % sectors) for i in range(sectors)])
    mate = lax.ppermute(mate, LON, [(i, i ^ 1) for i in range(sectors)])
    part = conv_call(block, top, bot, up, down, kernels)
    return part, mate, far


def start_copies(sources, targets, sems):
    copies = [
        pltpu.make_async_copy(src, dst, sems.at[i]) for i, (src, dst) in enumerate(zip(sources, targets))
    ]
    for copy in copies:
        copy.start()
    return copies


def load_kernel(block, count, *refs):
    sources = [
        ref if i < count - 4 else ref.at[block] for i, ref in enumerate(refs[:count])
    ]
    if block == 0:
        mask_ref, sea_ref = refs[count : count + 2]
        ids_ref, land_ref, sems = refs[-3:]
        targets = (ids_ref, land_ref) + tuple(refs[count + 2 : -3])
        copies = start_copies(sources, targets, sems)
        for copy in copies[:2]:
            copy.wait()
        for r in range(2):
            ids = jnp.broadcast_to(ids_ref[r : r + 1, :].astype(F32), (COLS, COLS))
            mask_ref[r] = (ids == ids.T).astype(F32)
            sea_ref[r] = jnp.broadcast_to(land_ref[r : r + 1, :].astype(F32), (COLS, COLS)).T
        copies = copies[2:]
    else:
        copies = start_copies(sources, refs[count:-1], refs[-1])
    for copy in copies:
        copy.wait()


def load_call(block, *arrays):
    count = len(arrays)
    shapes = [a.shape for a in arrays[:-4]] + [a.shape[1:] for a in arrays[-4:]]
    outs = [pltpu.VMEM(s, a.dtype) for s, a in zip(shapes, arrays)]
    scratch = [pltpu.SemaphoreType.DMA((count,))]
    if block == 0:
        outs = [pltpu.VMEM((2, COLS, COLS), F32)] * 2 + outs[2:]
        scratch = [pltpu.VMEM((2, COLS), jnp.int32), pltpu.VMEM((2, COLS), jnp.int32)] + scratch
    return pl.pallas_call(
        lambda *refs: load_kernel(block, count, *refs),
        out_shape=outs,
        in_specs=[ANY] * count,
        out_specs=[VM] * len(outs),
        scratch_shapes=scratch,
        compiler_params=PARAMS,
    )(*(pltpu.with_memory_space_constraint(a, pltpu.HBM) for a in arrays))


def per_device(atm_state, ocean_prev, land_sea, window_ids, conv_atm, attn_gain, qkv_matrix,
               attn_scales, out_matrix, mlp_gain, member_in, member_out, up_matrix, down_matrix,
               flux_matrix, conv_ocean, point_matrix, ocean_gain, ocean_qkv, ocean_scale, ocean_out,
               seaside_return_matrix):
    big = (qkv_matrix, out_matrix, up_matrix, down_matrix)
    mask, sea, conv_atm, attn_scales, attn_gain, mlp_gain, member_in, member_out, *weights = load_call(
        0, window_ids, land_sea, jnp.transpose(conv_atm, (1, 2, 0, 3)), attn_scales, attn_gain,
        mlp_gain, member_in, member_out, *big
    )
    small = (attn_gain, mlp_gain, member_in, member_out)
    part, mate, far = mix(0, atm_state[:, 0], atm_state[:, 1], conv_atm)
    top, bot = first_call(attn_scales, part, mate, far, mask, *small, *weights)

    (ocean_prev, flux_matrix, conv_ocean, point_matrix, ocean_gain, ocean_qkv, ocean_scale, ocean_out,
     seaside_return_matrix, *weights) = load_call(
        1, ocean_prev, flux_matrix, conv_ocean, point_matrix, ocean_gain[None, :], ocean_qkv,
        ocean_scale[None, :], ocean_out, seaside_return_matrix, *big
    )
    part, mate, far = mix(1, top, bot, conv_atm, ocean_scale)
    current, start = second_call(
        attn_scales, part, mate, far, mask, *small, *weights, ocean_prev, sea, flux_matrix
    )
    own = lax.all_to_all(start, "lat", 0, 0)
    axes = ("lat",) + LON
    pair = lax.ppermute(own, axes, group_swap(0))
    following = lax.ppermute(own, axes, group_swap(1))
    last = ocean_call(ocean_scale, own, pair, following, conv_ocean, point_matrix,
                      ocean_gain, ocean_qkv, ocean_out)
    last = lax.all_to_all(last, "lat", 0, 0)
    return final_call(last, start, current, sea, point_matrix, seaside_return_matrix)


def solution(mesh):
    field = P(None, "lat", LON, None)
    column = P("lat", LON)
    return jax.shard_map(
        per_device,
        mesh=mesh,
        in_specs=(field, field, column, column) + (P(),) * 18,
        out_specs=(field, field),
        check_vma=False,
    )
```

```python
import jax
import jax.numpy as jnp
from jax import lax
from jax.experimental import pallas as pl
from jax.experimental.pallas import tpu as pltpu
from jax.sharding import PartitionSpec as P


WIDTH = 384
HEADS = 6
HIDDEN = 1536
OCEAN = 128
COLS = 128
NORM_EPS = 1e-05
UNIT_EPS = 1e-06
LOG2E = 1.4426950408889634
STEP = 768
GROUP = 4
F32 = jnp.float32
BF16 = jnp.bfloat16
VM = pl.BlockSpec(memory_space=pltpu.VMEM)
SM = pl.BlockSpec(memory_space=pltpu.SMEM)
ANY = pl.BlockSpec(memory_space=pl.ANY)
PARAMS = pltpu.CompilerParams(vmem_limit_bytes=20 * 1024 * 1024)


def near(*arrays):
    return tuple(pltpu.with_memory_space_constraint(a, pltpu.VMEM) for a in arrays)


def dot(a, b):
    return jnp.dot(a, b, preferred_element_type=F32)


def dot_t(a, b):
    return lax.dot_general(a, b, (((1,), (1,)), ((), ())), preferred_element_type=F32)


def gelu(v):
    half = v * 0.5
    return half + half * lax.erf(v * 0.7071067811865476)


def norm_rows(x, gain):
    centred = x - jnp.mean(x, axis=-1, keepdims=True)
    spread = jnp.mean(centred * centred, axis=-1, keepdims=True)
    return centred * lax.rsqrt(spread + NORM_EPS) * gain


def head_mean(size):
    row = lax.broadcasted_iota(jnp.int32, (size, size), 0) // 64
    col = lax.broadcasted_iota(jnp.int32, (size, size), 1) // 64
    return jnp.where(row == col, 1.0 / 64.0, 0.0).astype(BF16)


def unit(p, mean_matrix):
    square = (p * p).astype(BF16)
    return (p * lax.rsqrt(dot(square, mean_matrix) + UNIT_EPS)).astype(BF16)


def pair_scores(q, k):
    low = lax.broadcasted_iota(jnp.int32, q.shape, 1) < 64
    zero = jnp.zeros_like(q)
    return dot_t(jnp.concatenate([jnp.where(low, q, zero), jnp.where(low, zero, q)], axis=0), k)


def pair_terms(scores, mask, scale_even, scale_odd):
    rows = scores.shape[0] // 2
    even = jnp.exp2(scores[:rows] * scale_even) * mask
    odd = jnp.exp2(scores[rows:] * scale_odd) * mask
    return jnp.concatenate([even, odd], axis=0).astype(BF16)


def pair_result(terms, v):
    rows = v.shape[0]
    low = lax.broadcasted_iota(jnp.int32, v.shape, 1) < 64
    sums = dot(terms, jnp.concatenate([v, jnp.ones_like(v)], axis=1))
    number = jnp.where(low, sums[:rows, :128], sums[rows:, :128])
    denom = jnp.where(low, sums[:rows, 128:], sums[rows:, 128:])
    return (number / denom).astype(BF16)


def pair_attend(q, k, v, mask, scale_even, scale_odd):
    return pair_result(pair_terms(pair_scores(q, k), mask, scale_even, scale_odd), v)


def shift_cols(t, step, axis):
    return pltpu.roll(t, step % t.shape[axis], axis)


def edge_kernel(block, top_ref, bot_ref, up_ref, down_ref, k_ref, *refs):
    mate_ref, far_ref = refs[-2:]
    has_up, has_down = inner_rows()
    even = lax.axis_index("comp") == 0

    def tap(i, j):
        return k_ref[i, j, block : block + 1, :]

    for m in range(2):
        def column(c):
            return [
                up_ref[m, c : c + 1, :].astype(F32) * has_up,
                top_ref[m, c : c + 1, :].astype(F32),
                bot_ref[m, c : c + 1, :].astype(F32),
                down_ref[m, c : c + 1, :].astype(F32) * has_down,
            ]

        final, first = column(COLS - 1), column(0)
        for r in range(2):
            right = sum(tap(i, 0) * final[r + i] for i in range(3))
            left = sum(tap(i, 2) * first[r + i] for i in range(3))
            i = 2 * m + r
            mate_ref[i : i + 1, :] = jnp.where(even, right, left)
            far_ref[i : i + 1, :] = jnp.where(even, left, right)


def inner_rows():
    lat = lax.axis_index("lat")
    return (lat > 0).astype(F32), (lat < lax.axis_size("lat") - 1).astype(F32)


def project(mixed, gain, qkv):
    mean_matrix = head_mean(256)
    out = dot(norm_rows(mixed, gain).astype(BF16), qkv)
    units = [unit(out[:, 256 * i : 256 * i + 256], mean_matrix) for i in range(3)]
    return jnp.concatenate(units + [out[:, 2 * WIDTH :].astype(BF16)], axis=1)


def conv_kernel(block, top_ref, bot_ref, up_ref, down_ref, k_ref, gain_ref, qkv_ref, mixed_ref,
                units_ref, ends_ref):
    has_up, has_down = inner_rows()
    first_col = lax.broadcasted_iota(jnp.int32, (COLS, WIDTH), 0) == 0
    final_col = lax.broadcasted_iota(jnp.int32, (COLS, WIDTH), 0) == COLS - 1

    def tap(i, j):
        return k_ref[i, j, block : block + 1, :]

    parts = []
    for m in range(2):
        rows = [
            up_ref[m].astype(F32) * has_up,
            top_ref[m].astype(F32),
            bot_ref[m].astype(F32),
            down_ref[m].astype(F32) * has_down,
        ]
        for r in range(2):
            a, b, c = rows[r : r + 3]
            mid = tap(0, 1) * a + (tap(1, 1) + 1.0) * b + tap(2, 1) * c
            west = tap(0, 0) * a + tap(1, 0) * b + tap(2, 0) * c
            east = tap(0, 2) * a + tap(1, 2) * b + tap(2, 2) * c
            part = (
                mid
                + jnp.where(first_col, 0.0, shift_cols(west, 1, 0))
                + jnp.where(final_col, 0.0, shift_cols(east, -1, 0))
            )
            i = 2 * m + r
            ends_ref[i : i + 1, :] = part[:1]
            ends_ref[4 + i : 5 + i, :] = part[COLS - 1 :]
            parts.append(part.astype(BF16))
    mixed = jnp.concatenate(parts, axis=0)
    mixed_ref[...] = mixed
    units_ref[...] = project(mixed.astype(F32), gain_ref[block : block + 1, :], qkv_ref[...])


def edge_call(block, *args):
    return pl.pallas_call(
        lambda *refs: edge_kernel(block, *refs),
        out_shape=(pltpu.VMEM((4, WIDTH), F32), pltpu.VMEM((4, WIDTH), F32)),
        in_specs=[VM] * len(args),
        out_specs=(VM, VM),
        compiler_params=PARAMS,
    )(*near(*args))


def conv_call(block, *args):
    return pl.pallas_call(
        lambda *refs: conv_kernel(block, *refs),
        out_shape=(
            pltpu.VMEM((4 * COLS, WIDTH), BF16),
            pltpu.VMEM((4 * COLS, 3 * WIDTH), BF16),
            pltpu.VMEM((8, WIDTH), F32),
        ),
        in_specs=[VM] * 7,
        out_specs=(VM,) * 3,
        compiler_params=PARAMS,
    )(*near(*args))


def patched(ref, ends, i):
    at = lax.broadcasted_iota(jnp.int32, (16, ref.shape[1]), 0)
    low = jnp.where(at == 0, ends[i : i + 1], ref[COLS * i : COLS * i + 16, :].astype(F32))
    high = jnp.where(
        at == 15, ends[4 + i : 5 + i], ref[COLS * i + 112 : COLS * i + 128, :].astype(F32)
    )
    middle = ref[COLS * i + 16 : COLS * i + 112, :]
    return jnp.concatenate([low.astype(BF16), middle, high.astype(BF16)], axis=0)


def block_body(block, scale_ref, mixed_ref, units_ref, ends_ref, mate_ref, far_ref, mask_ref, gain_ref,
               mlp_gain_ref, min_ref, mout_ref, weights, store):
    qkv_ref, out_ref, up_ref, down_ref = weights
    even = lax.axis_index("comp") == 0
    mate, far = mate_ref[...], far_ref[...]
    first = ends_ref[:4] + jnp.where(even, far, mate)
    final = ends_ref[4:] + jnp.where(even, mate, far)
    ends = jnp.concatenate([first, final, first, final], axis=0).astype(BF16).astype(F32)
    end_units = project(ends, gain_ref[block : block + 1, :], qkv_ref()).astype(F32)
    units = [patched(units_ref, end_units, i) for i in range(4)]
    mixed = jnp.concatenate([patched(mixed_ref, ends, i) for i in range(4)], axis=0).astype(F32)

    scales = [
        scale_ref[block : block + 1, h : h + 1] * (LOG2E / 64) for h in range(HEADS)
    ]
    row_out = []
    for first in range(0, 4, GROUP):
        cells = [(i, j) for i in range(first, first + GROUP) for j in range(3)]
        lanes = [slice(128 * j, 128 * j + 128) for j in range(9)]
        scores = [pair_scores(units[i][:, lanes[j]], units[i][:, lanes[3 + j]]) for i, j in cells]
        terms = [
            pair_terms(x, mask_ref[i % 2], scales[2 * j], scales[2 * j + 1])
            for x, (i, j) in zip(scores, cells)
        ]
        results = [
            pair_result(t, units[i][:, lanes[6 + j]]) for t, (i, j) in zip(terms, cells)
        ]
        for i in range(GROUP):
            row_out.append(jnp.concatenate(results[3 * i : 3 * i + 3], axis=1))
    attended = jnp.concatenate(row_out, axis=0)
    after = (mixed + dot(attended, out_ref())).astype(BF16)
    after_f = after.astype(F32)
    scaled = norm_rows(after_f, mlp_gain_ref[block : block + 1, :])
    scaled = jnp.concatenate(
        [
            (scaled[: 2 * COLS] * min_ref[block, 0:1, :]).astype(BF16),
            (scaled[2 * COLS :] * min_ref[block, 1:2, :]).astype(BF16),
        ],
        axis=0,
    )
    total = after_f
    for h in range(0, HIDDEN, STEP):
        lifted = dot(scaled, up_ref(h, STEP))
        active = jnp.concatenate(
            [
                gelu(lifted[: 2 * COLS] * mout_ref[block, 0:1, h : h + STEP]).astype(BF16),
                gelu(lifted[2 * COLS :] * mout_ref[block, 1:2, h : h + STEP]).astype(BF16),
            ],
            axis=0,
        )
        total = total + dot(active, down_ref(h, STEP))
    store(total.astype(BF16))


def weight_getters(refs):
    return (
        lambda: refs[0][...],
        lambda: refs[1][...],
        lambda h, n: refs[2][:, h : h + n],
        lambda h, n: refs[3][h : h + n, :],
    )


def first_kernel(scale_ref, mixed_ref, units_ref, ends_ref, mate_ref, far_ref, mask_ref, gain_ref, mlp_gain_ref, min_ref,
                 mout_ref, qkv_h, out_h, up_h, down_h, top_ref, bot_ref):
    weights = weight_getters((qkv_h, out_h, up_h, down_h))

    def store(value):
        for m in range(2):
            top_ref[m] = value[2 * m * COLS : (2 * m + 1) * COLS]
            bot_ref[m] = value[(2 * m + 1) * COLS : (2 * m + 2) * COLS]

    block_body(0, scale_ref, mixed_ref, units_ref, ends_ref, mate_ref, far_ref, mask_ref, gain_ref, mlp_gain_ref,
               min_ref, mout_ref, weights, store)


def turned(value, straight):
    back = jnp.concatenate([value[j : j + 1] for j in reversed(range(value.shape[0]))], axis=0)
    return jnp.where(straight, value, back)


def second_kernel(scale_ref, mixed_ref, units_ref, ends_ref, mate_ref, far_ref, mask_ref, gain_ref, mlp_gain_ref, min_ref,
                  mout_ref, qkv_h, out_h, up_h, down_h, prev_ref, sea_ref, flux_ref,
                  cur_ref, start_ref):
    weights = weight_getters((qkv_h, out_h, up_h, down_h))

    straight = lax.axis_index("comp") == 0

    def store(value):
        flux = dot(value, flux_ref[...])
        for i in range(4):
            m, r = i // 2, i % 2
            at = slice(COLS * i, COLS * i + COLS)
            cur_ref[m, r] = value[at]
            start = sea_ref[r] * (prev_ref[m, r].astype(F32) + flux[at])
            start_ref[:, i] = turned(start.reshape(16, 8, OCEAN), straight).astype(BF16)

    block_body(1, scale_ref, mixed_ref, units_ref, ends_ref, mate_ref, far_ref, mask_ref, gain_ref, mlp_gain_ref,
               min_ref, mout_ref, weights, store)


def first_call(*args):
    row = pltpu.VMEM((2, COLS, WIDTH), BF16)
    return pl.pallas_call(
        first_kernel,
        out_shape=(row, row),
        in_specs=[VM] * 15,
        out_specs=(VM, VM),
        compiler_params=PARAMS,
        name="block_0",
    )(*near(*args))


def second_call(*args):
    return pl.pallas_call(
        second_kernel,
        out_shape=(
            pltpu.VMEM((2, 2, COLS, WIDTH), BF16),
            pltpu.VMEM((16, 4, 8, OCEAN), BF16),
        ),
        in_specs=[VM] * 18,
        out_specs=(VM, VM),
        compiler_params=PARAMS,
        name="block_1",
    )(*near(*args))


def taps3(columns, k_ref, index):
    total = 0.0
    for j, field in enumerate(columns):
        zero = jnp.zeros_like(field[:1])
        above = jnp.concatenate([zero, field[:-1]], axis=0)
        below = jnp.concatenate([field[1:], zero], axis=0)
        total = total + (
            k_ref[index, 0, j : j + 1, :] * above
            + k_ref[index, 1, j : j + 1, :] * field
            + k_ref[index, 2, j : j + 1, :] * below
        )
    return total


def ocean_kernel(scale_ref, own_ref, pair_ref, next_ref, k_ref, point_ref, gain_ref, qkv_ref,
                 out_ref, last_ref, field_ref, pool_ref, wide_ref, merged_ref):
    mean_matrix = head_mean(128)
    row = lax.broadcasted_iota(jnp.int32, (128, 128), 0) % 8
    col = lax.broadcasted_iota(jnp.int32, (128, 128), 1) % 8
    mask = jnp.where(row == col, 1.0, 0.0)
    first_of_pair = (lax.axis_index("lat") + lax.axis_index("comp")) % 2 == 0
    fine_all = []
    for m in range(2):
        def rows_of(ref):
            even = ref[:, 2 * m].astype(F32)[:, None]
            odd = ref[:, 2 * m + 1].astype(F32)[:, None]
            return jnp.concatenate([even, odd], axis=1).reshape(32, 8, OCEAN)

        pair = rows_of(pair_ref)
        following = rows_of(next_ref)
        field_ref[m, :, 0:8, :] = jnp.where(first_of_pair, following, pair)
        field_ref[m, :, 8:16, :] = rows_of(own_ref)
        field_ref[m, :, 16:24, :] = jnp.where(first_of_pair, pair, following)
        act = taps3([field_ref[m, :, 3 + j : 19 + j, :] for j in range(3)], k_ref, 0)
        act = act.astype(BF16).reshape(32 * 16, OCEAN)
        fine = gelu(dot(act, point_ref[0])).astype(BF16).astype(F32).reshape(16, 2, 16, OCEAN)
        fine_all.append(fine)
        pool_ref[m] = (fine[:, 0] + fine[:, 1]).reshape(256, OCEAN)
    coarse = []
    for m in range(2):
        pooled = pool_ref[m, pl.ds(0, 128, stride=2), :] + pool_ref[m, pl.ds(1, 128, stride=2), :]
        coarse.append((pooled * 0.25).astype(BF16).astype(F32).reshape(16, 8, OCEAN))
    acts = []
    for m in range(2):
        columns = (shift_cols(coarse[m], 1, 1), coarse[m], shift_cols(coarse[m], -1, 1))
        acts.append(taps3(columns, k_ref, 1).astype(BF16).reshape(128, OCEAN))
    first = gelu(dot(jnp.concatenate(acts, axis=0), point_ref[1])).astype(BF16).astype(F32)
    normed = norm_rows(first, gain_ref[...]).astype(BF16)
    qkv = dot(normed, qkv_ref[...])
    query = unit(qkv[:, :128], mean_matrix)
    key = unit(qkv[:, 128:256], mean_matrix)
    value = qkv[:, 256:].astype(BF16)
    attended = []
    for m in range(2):
        at = slice(128 * m, 128 * m + 128)
        attended.append(
            pair_attend(
                query[at],
                key[at],
                value[at],
                mask,
                scale_ref[:, 0:1] * (LOG2E / 64),
                scale_ref[:, 1:2] * (LOG2E / 64),
            )
        )
    attended = jnp.concatenate(attended, axis=0)
    coarse_next = (first + dot(attended, out_ref[...])).astype(BF16).astype(F32)
    for m in range(2):
        piece = coarse_next[128 * m : 128 * m + 128]
        wide_ref[m, pl.ds(0, 128, stride=2), :] = piece
        wide_ref[m, pl.ds(1, 128, stride=2), :] = piece
    for m in range(2):
        spread = wide_ref[m].reshape(16, 1, 16, OCEAN)
        merged_ref[m] = (fine_all[m] + spread).astype(BF16).astype(F32).reshape(32, 16, OCEAN)
        act = taps3([merged_ref[m, :, 3 + j : 11 + j, :] for j in range(3)], k_ref, 2)
        act = act.astype(BF16).reshape(16, 2, 8, OCEAN)
        last_ref[:, 2 * m] = act[:, 0]
        last_ref[:, 2 * m + 1] = act[:, 1]


def ocean_call(*args):
    return pl.pallas_call(
        ocean_kernel,
        out_shape=pltpu.VMEM((16, 4, 8, OCEAN), BF16),
        in_specs=[VM] * 9,
        out_specs=VM,
        compiler_params=PARAMS,
        scratch_shapes=[
            pltpu.VMEM((2, 32, 24, OCEAN), F32),
            pltpu.VMEM((2, 256, OCEAN), F32),
            pltpu.VMEM((2, 256, OCEAN), F32),
            pltpu.VMEM((2, 32, 16, OCEAN), F32),
        ],
        name="ocean",
    )(*near(*args))


def final_kernel(last_ref, start_ref, cur_ref, sea_ref, point_ref, return_ref, air_hbm, water_hbm,
                 air_ref, water_ref, sems):
    copies = []

    def send(src, dst, m, r, k):
        copies.append(pltpu.make_async_copy(src.at[m, r], dst.at[m, r], sems.at[k]))
        copies[-1].start()

    straight = lax.axis_index("comp") == 0
    acts = [
        turned(last_ref[:, i].astype(F32), straight).astype(BF16).reshape(COLS, OCEAN) for i in range(4)
    ]
    lifted = gelu(dot(jnp.concatenate(acts, axis=0), point_ref[2]))
    waters = []
    for i in range(4):
        m, r = i // 2, i % 2
        start = turned(start_ref[:, i].astype(F32), straight).reshape(COLS, OCEAN)
        waters.append((sea_ref[r] * (start + lifted[COLS * i : COLS * i + COLS])).astype(BF16))
        water_ref[m, r] = waters[i]
        send(water_ref, water_hbm, m, r, i)
    back = dot(jnp.concatenate(waters, axis=0), return_ref[...])
    for i in range(4):
        m, r = i // 2, i % 2
        sea = jnp.concatenate([sea_ref[r]] * 3, axis=1)
        air_ref[m, r] = (cur_ref[m, r].astype(F32) + sea * back[COLS * i : COLS * i + COLS]).astype(BF16)
        send(air_ref, air_hbm, m, r, 4 + i)
    for copy in copies:
        copy.wait()


def final_call(*args):
    return pl.pallas_call(
        final_kernel,
        out_shape=(
            jax.ShapeDtypeStruct((2, 2, COLS, WIDTH), BF16),
            jax.ShapeDtypeStruct((2, 2, COLS, OCEAN), BF16),
        ),
        in_specs=[VM] * 6,
        out_specs=(ANY, ANY),
        scratch_shapes=[
            pltpu.VMEM((2, 2, COLS, WIDTH), BF16),
            pltpu.VMEM((2, 2, COLS, OCEAN), BF16),
            pltpu.SemaphoreType.DMA((8,)),
        ],
        compiler_params=PARAMS,
        name="final",
    )(*near(*args))


LON = ("lon", "comp")


def ring(count, step):
    return [(i, (i + step) % count) for i in range(count)]


def group_swap(first):
    lats = lax.axis_size("lat")
    sectors = lax.axis_size("lon") * lax.axis_size("comp")
    total = lats * sectors

    def device(g):
        sector, place = g // lats, g % lats
        lat = place if sector % 2 == 0 else lats - 1 - place
        return lat * sectors + sector

    pairs = []
    for g in range(first, total, 2):
        a, b = device(g), device((g + 1) % total)
        pairs += [(a, b), (b, a)]
    return sorted(pairs)


def mix(block, top, bot, kernels, gain, qkv, *after):
    lats = lax.axis_size("lat")
    sectors = lax.axis_size("lon") * lax.axis_size("comp")
    up = lax.ppermute(bot, "lat", ring(lats, 1))
    down = lax.ppermute(top, "lat", ring(lats, -1))
    mate, far = edge_call(block, top, bot, up, down, kernels, *after)
    far = lax.ppermute(far, LON, [(i, (i + 2 * (i % 2) - 1) % sectors) for i in range(sectors)])
    mate = lax.ppermute(mate, LON, [(i, i ^ 1) for i in range(sectors)])
    part = conv_call(block, top, bot, up, down, kernels, gain, qkv)
    return (*part, mate, far)


def start_copies(sources, targets, sems):
    copies = [
        pltpu.make_async_copy(src, dst, sems.at[i]) for i, (src, dst) in enumerate(zip(sources, targets))
    ]
    for copy in copies:
        copy.start()
    return copies


def load_kernel(block, count, *refs):
    sources = [
        ref if i < count - 4 else ref.at[block] for i, ref in enumerate(refs[:count])
    ]
    if block == 0:
        mask_ref, sea_ref = refs[count : count + 2]
        ids_ref, land_ref, sems = refs[-3:]
        targets = (ids_ref, land_ref) + tuple(refs[count + 2 : -3])
        copies = start_copies(sources, targets, sems)
        for copy in copies[:2]:
            copy.wait()
        for r in range(2):
            ids = jnp.broadcast_to(ids_ref[r : r + 1, :].astype(F32), (COLS, COLS))
            mask_ref[r] = (ids == ids.T).astype(F32)
            sea_ref[r] = jnp.broadcast_to(land_ref[r : r + 1, :].astype(F32), (COLS, COLS)).T
        copies = copies[2:]
    else:
        copies = start_copies(sources, refs[count:-1], refs[-1])
    for copy in copies:
        copy.wait()


def load_call(block, *arrays):
    count = len(arrays)
    shapes = [a.shape for a in arrays[:-4]] + [a.shape[1:] for a in arrays[-4:]]
    outs = [pltpu.VMEM(s, a.dtype) for s, a in zip(shapes, arrays)]
    scratch = [pltpu.SemaphoreType.DMA((count,))]
    if block == 0:
        outs = [pltpu.VMEM((2, COLS, COLS), F32)] * 2 + outs[2:]
        scratch = [pltpu.VMEM((2, COLS), jnp.int32), pltpu.VMEM((2, COLS), jnp.int32)] + scratch
    return pl.pallas_call(
        lambda *refs: load_kernel(block, count, *refs),
        out_shape=outs,
        in_specs=[ANY] * count,
        out_specs=[VM] * len(outs),
        scratch_shapes=scratch,
        compiler_params=PARAMS,
    )(*(pltpu.with_memory_space_constraint(a, pltpu.HBM) for a in arrays))


def per_device(atm_state, ocean_prev, land_sea, window_ids, conv_atm, attn_gain, qkv_matrix,
               attn_scales, out_matrix, mlp_gain, member_in, member_out, up_matrix, down_matrix,
               flux_matrix, conv_ocean, point_matrix, ocean_gain, ocean_qkv, ocean_scale, ocean_out,
               seaside_return_matrix):
    big = (qkv_matrix, out_matrix, up_matrix, down_matrix)
    mask, sea, conv_atm, attn_scales, attn_gain, mlp_gain, member_in, member_out, *weights = load_call(
        0, window_ids, land_sea, jnp.transpose(conv_atm, (1, 2, 0, 3)), attn_scales, attn_gain,
        mlp_gain, member_in, member_out, *big
    )
    small = (attn_gain, mlp_gain, member_in, member_out)
    mixed = mix(0, atm_state[:, 0], atm_state[:, 1], conv_atm, attn_gain, weights[0])
    top, bot = first_call(attn_scales, *mixed, mask, *small, *weights)

    (ocean_prev, flux_matrix, conv_ocean, point_matrix, ocean_gain, ocean_qkv, ocean_scale, ocean_out,
     seaside_return_matrix, *weights) = load_call(
        1, ocean_prev, flux_matrix, conv_ocean, point_matrix, ocean_gain[None, :], ocean_qkv,
        ocean_scale[None, :], ocean_out, seaside_return_matrix, *big
    )
    mixed = mix(1, top, bot, conv_atm, attn_gain, weights[0], ocean_scale)
    current, start = second_call(
        attn_scales, *mixed, mask, *small, *weights, ocean_prev, sea, flux_matrix
    )
    own = lax.all_to_all(start, "lat", 0, 0)
    axes = ("lat",) + LON
    pair = lax.ppermute(own, axes, group_swap(0))
    following = lax.ppermute(own, axes, group_swap(1))
    last = ocean_call(ocean_scale, own, pair, following, conv_ocean, point_matrix,
                      ocean_gain, ocean_qkv, ocean_out)
    last = lax.all_to_all(last, "lat", 0, 0)
    return final_call(last, start, current, sea, point_matrix, seaside_return_matrix)


def solution(mesh):
    field = P(None, "lat", LON, None)
    column = P("lat", LON)
    return jax.shard_map(
        per_device,
        mesh=mesh,
        in_specs=(field, field, column, column) + (P(),) * 18,
        out_specs=(field, field),
        check_vma=False,
    )
```

```python
import jax
import jax.numpy as jnp
from jax import lax
from jax.experimental import pallas as pl
from jax.experimental.pallas import tpu as pltpu
from jax.sharding import PartitionSpec as P


WIDTH = 384
HEADS = 6
HIDDEN = 1536
OCEAN = 128
COLS = 128
NORM_EPS = 1e-05
UNIT_EPS = 1e-06
LOG2E = 1.4426950408889634
STEP = 768
GROUP = 4
F32 = jnp.float32
BF16 = jnp.bfloat16
VM = pl.BlockSpec(memory_space=pltpu.VMEM)
SM = pl.BlockSpec(memory_space=pltpu.SMEM)
ANY = pl.BlockSpec(memory_space=pl.ANY)
PARAMS = pltpu.CompilerParams(vmem_limit_bytes=20 * 1024 * 1024)
BLOCK_PARAMS = pltpu.CompilerParams(vmem_limit_bytes=20 * 1024 * 1024)


def near(*arrays):
    return tuple(pltpu.with_memory_space_constraint(a, pltpu.VMEM) for a in arrays)


def dot(a, b):
    return jnp.dot(a, b, preferred_element_type=F32)


def dot_t(a, b):
    return lax.dot_general(a, b, (((1,), (1,)), ((), ())), preferred_element_type=F32)


def gelu(v):
    half = v * 0.5
    return half + half * lax.erf(v * 0.7071067811865476)


def norm_rows(x, gain):
    centred = x - jnp.mean(x, axis=-1, keepdims=True)
    spread = jnp.mean(centred * centred, axis=-1, keepdims=True)
    return centred * lax.rsqrt(spread + NORM_EPS) * gain


def head_mean(size):
    row = lax.broadcasted_iota(jnp.int32, (size, size), 0) // 64
    col = lax.broadcasted_iota(jnp.int32, (size, size), 1) // 64
    return jnp.where(row == col, 1.0 / 64.0, 0.0).astype(BF16)


def unit(p, mean_matrix):
    square = (p * p).astype(BF16)
    return (p * lax.rsqrt(dot(square, mean_matrix) + UNIT_EPS)).astype(BF16)


def pair_scores(q, k):
    low = lax.broadcasted_iota(jnp.int32, q.shape, 1) < 64
    zero = jnp.zeros_like(q)
    return dot_t(jnp.concatenate([jnp.where(low, q, zero), jnp.where(low, zero, q)], axis=0), k)


def pair_terms(scores, mask, scale_even, scale_odd):
    rows = scores.shape[0] // 2
    even = jnp.exp2(scores[:rows] * scale_even) * mask
    odd = jnp.exp2(scores[rows:] * scale_odd) * mask
    return jnp.concatenate([even, odd], axis=0).astype(BF16)


def pair_result(terms, v):
    rows = v.shape[0]
    low = lax.broadcasted_iota(jnp.int32, v.shape, 1) < 64
    sums = dot(terms, jnp.concatenate([v, jnp.ones_like(v)], axis=1))
    number = jnp.where(low, sums[:rows, :128], sums[rows:, :128])
    denom = jnp.where(low, sums[:rows, 128:], sums[rows:, 128:])
    return (number / denom).astype(BF16)


def pair_attend(q, k, v, mask, scale_even, scale_odd):
    return pair_result(pair_terms(pair_scores(q, k), mask, scale_even, scale_odd), v)


def shift_cols(t, step, axis):
    return pltpu.roll(t, step % t.shape[axis], axis)


def edge_kernel(block, top_ref, bot_ref, up_ref, down_ref, k_ref, *refs):
    mate_ref, far_ref = refs[-2:]
    has_up, has_down = inner_rows()
    even = lax.axis_index("comp") == 0

    def tap(i, j):
        return k_ref[i, j, block : block + 1, :]

    for m in range(2):
        def column(c):
            return [
                up_ref[m, c : c + 1, :].astype(F32) * has_up,
                top_ref[m, c : c + 1, :].astype(F32),
                bot_ref[m, c : c + 1, :].astype(F32),
                down_ref[m, c : c + 1, :].astype(F32) * has_down,
            ]

        final, first = column(COLS - 1), column(0)
        for r in range(2):
            right = sum(tap(i, 0) * final[r + i] for i in range(3))
            left = sum(tap(i, 2) * first[r + i] for i in range(3))
            i = 2 * m + r
            mate_ref[i : i + 1, :] = jnp.where(even, right, left)
            far_ref[i : i + 1, :] = jnp.where(even, left, right)


def inner_rows():
    lat = lax.axis_index("lat")
    return (lat > 0).astype(F32), (lat < lax.axis_size("lat") - 1).astype(F32)


def project(mixed, gain, qkv):
    mean_matrix = head_mean(256)
    out = dot(norm_rows(mixed, gain).astype(BF16), qkv)
    units = [unit(out[:, 256 * i : 256 * i + 256], mean_matrix) for i in range(3)]
    return jnp.concatenate(units + [out[:, 2 * WIDTH :].astype(BF16)], axis=1)


def conv_kernel(block, top_ref, bot_ref, up_ref, down_ref, k_ref, gain_ref, qkv_ref, mixed_ref,
                units_ref, ends_ref):
    has_up, has_down = inner_rows()
    first_col = lax.broadcasted_iota(jnp.int32, (COLS, WIDTH), 0) == 0
    final_col = lax.broadcasted_iota(jnp.int32, (COLS, WIDTH), 0) == COLS - 1

    def tap(i, j):
        return k_ref[i, j, block : block + 1, :]

    parts = []
    for m in range(2):
        rows = [
            up_ref[m].astype(F32) * has_up,
            top_ref[m].astype(F32),
            bot_ref[m].astype(F32),
            down_ref[m].astype(F32) * has_down,
        ]
        for r in range(2):
            a, b, c = rows[r : r + 3]
            mid = tap(0, 1) * a + (tap(1, 1) + 1.0) * b + tap(2, 1) * c
            west = tap(0, 0) * a + tap(1, 0) * b + tap(2, 0) * c
            east = tap(0, 2) * a + tap(1, 2) * b + tap(2, 2) * c
            part = (
                mid
                + jnp.where(first_col, 0.0, shift_cols(west, 1, 0))
                + jnp.where(final_col, 0.0, shift_cols(east, -1, 0))
            )
            i = 2 * m + r
            ends_ref[i : i + 1, :] = part[:1]
            ends_ref[4 + i : 5 + i, :] = part[COLS - 1 :]
            parts.append(part.astype(BF16))
    mixed = jnp.concatenate(parts, axis=0)
    mixed_ref[...] = mixed
    units_ref[...] = project(mixed.astype(F32), gain_ref[block : block + 1, :], qkv_ref[...])


def edge_call(block, *args):
    return pl.pallas_call(
        lambda *refs: edge_kernel(block, *refs),
        out_shape=(pltpu.VMEM((4, WIDTH), F32), pltpu.VMEM((4, WIDTH), F32)),
        in_specs=[VM] * len(args),
        out_specs=(VM, VM),
        compiler_params=PARAMS,
    )(*near(*args))


def conv_call(block, *args):
    return pl.pallas_call(
        lambda *refs: conv_kernel(block, *refs),
        out_shape=(
            pltpu.VMEM((4 * COLS, WIDTH), BF16),
            pltpu.VMEM((4 * COLS, 3 * WIDTH), BF16),
            pltpu.VMEM((8, WIDTH), F32),
        ),
        in_specs=[VM] * 7,
        out_specs=(VM,) * 3,
        compiler_params=PARAMS,
    )(*near(*args))


def patched(ref, ends, i):
    at = lax.broadcasted_iota(jnp.int32, (16, ref.shape[1]), 0)
    low = jnp.where(at == 0, ends[i : i + 1], ref[COLS * i : COLS * i + 16, :].astype(F32))
    high = jnp.where(
        at == 15, ends[4 + i : 5 + i], ref[COLS * i + 112 : COLS * i + 128, :].astype(F32)
    )
    middle = ref[COLS * i + 16 : COLS * i + 112, :]
    return jnp.concatenate([low.astype(BF16), middle, high.astype(BF16)], axis=0)


def block_body(block, scale_ref, mixed_ref, units_ref, ends_ref, mate_ref, far_ref, mask_ref, gain_ref,
               mlp_gain_ref, min_ref, mout_ref, weights, store):
    qkv_ref, out_ref, up_ref, down_ref = weights
    even = lax.axis_index("comp") == 0
    mate, far = mate_ref[...], far_ref[...]
    first = ends_ref[:4] + jnp.where(even, far, mate)
    final = ends_ref[4:] + jnp.where(even, mate, far)
    ends = jnp.concatenate([first, final, first, final], axis=0).astype(BF16).astype(F32)
    end_units = project(ends, gain_ref[block : block + 1, :], qkv_ref()).astype(F32)
    units = [patched(units_ref, end_units, i) for i in range(4)]
    mixed = jnp.concatenate([patched(mixed_ref, ends, i) for i in range(4)], axis=0).astype(F32)

    scales = [
        scale_ref[block : block + 1, h : h + 1] * (LOG2E / 64) for h in range(HEADS)
    ]
    row_out = []
    for first in range(0, 4, GROUP):
        cells = [(i, j) for i in range(first, first + GROUP) for j in range(3)]
        lanes = [slice(128 * j, 128 * j + 128) for j in range(9)]
        scores = [pair_scores(units[i][:, lanes[j]], units[i][:, lanes[3 + j]]) for i, j in cells]
        terms = [
            pair_terms(x, mask_ref[i % 2], scales[2 * j], scales[2 * j + 1])
            for x, (i, j) in zip(scores, cells)
        ]
        results = [
            pair_result(t, units[i][:, lanes[6 + j]]) for t, (i, j) in zip(terms, cells)
        ]
        for i in range(GROUP):
            row_out.append(jnp.concatenate(results[3 * i : 3 * i + 3], axis=1))
    attended = jnp.concatenate(row_out, axis=0)
    after = (mixed + dot(attended, out_ref())).astype(BF16)
    after_f = after.astype(F32)
    scaled = norm_rows(after_f, mlp_gain_ref[block : block + 1, :])
    scaled = jnp.concatenate(
        [
            (scaled[: 2 * COLS] * min_ref[block, 0:1, :]).astype(BF16),
            (scaled[2 * COLS :] * min_ref[block, 1:2, :]).astype(BF16),
        ],
        axis=0,
    )
    total = after_f
    for h in range(0, HIDDEN, STEP):
        lifted = dot(scaled, up_ref(h, STEP))
        active = jnp.concatenate(
            [
                gelu(lifted[: 2 * COLS] * mout_ref[block, 0:1, h : h + STEP]).astype(BF16),
                gelu(lifted[2 * COLS :] * mout_ref[block, 1:2, h : h + STEP]).astype(BF16),
            ],
            axis=0,
        )
        total = total + dot(active, down_ref(h, STEP))
    store(total.astype(BF16))


def weight_getters(refs):
    return (
        lambda: refs[0][...],
        lambda: refs[1][...],
        lambda h, n: refs[2][:, h : h + n],
        lambda h, n: refs[3][h : h + n, :],
    )


def first_kernel(scale_ref, mixed_ref, units_ref, ends_ref, mate_ref, far_ref, mask_ref, gain_ref, mlp_gain_ref, min_ref,
                 mout_ref, qkv_h, out_h, up_h, down_h, top_ref, bot_ref):
    weights = weight_getters((qkv_h, out_h, up_h, down_h))

    def store(value):
        for m in range(2):
            top_ref[m] = value[2 * m * COLS : (2 * m + 1) * COLS]
            bot_ref[m] = value[(2 * m + 1) * COLS : (2 * m + 2) * COLS]

    block_body(0, scale_ref, mixed_ref, units_ref, ends_ref, mate_ref, far_ref, mask_ref, gain_ref, mlp_gain_ref,
               min_ref, mout_ref, weights, store)


def turned(value, straight):
    back = jnp.concatenate([value[j : j + 1] for j in reversed(range(value.shape[0]))], axis=0)
    return jnp.where(straight, value, back)


def second_kernel(scale_ref, mixed_ref, units_ref, ends_ref, mate_ref, far_ref, mask_ref, gain_ref, mlp_gain_ref, min_ref,
                  mout_ref, qkv_h, out_h, up_h, down_h, prev_ref, sea_ref, flux_ref,
                  cur_ref, start_ref):
    weights = weight_getters((qkv_h, out_h, up_h, down_h))

    straight = lax.axis_index("comp") == 0

    def store(value):
        flux = dot(value, flux_ref[...])
        for i in range(4):
            m, r = i // 2, i % 2
            at = slice(COLS * i, COLS * i + COLS)
            cur_ref[m, r] = value[at]
            start = sea_ref[r] * (prev_ref[m, r].astype(F32) + flux[at])
            start_ref[:, i] = turned(start.reshape(16, 8, OCEAN), straight).astype(BF16)

    block_body(1, scale_ref, mixed_ref, units_ref, ends_ref, mate_ref, far_ref, mask_ref, gain_ref, mlp_gain_ref,
               min_ref, mout_ref, weights, store)


def first_call(*args):
    row = pltpu.VMEM((2, COLS, WIDTH), BF16)
    return pl.pallas_call(
        first_kernel,
        out_shape=(row, row),
        in_specs=[VM] * 15,
        out_specs=(VM, VM),
        compiler_params=BLOCK_PARAMS,
        name="block_0",
    )(*near(*args))


def second_call(*args):
    return pl.pallas_call(
        second_kernel,
        out_shape=(
            pltpu.VMEM((2, 2, COLS, WIDTH), BF16),
            pltpu.VMEM((16, 4, 8, OCEAN), BF16),
        ),
        in_specs=[VM] * 18,
        out_specs=(VM, VM),
        compiler_params=BLOCK_PARAMS,
        name="block_1",
    )(*near(*args))


def taps3(columns, k_ref, index):
    total = 0.0
    for j, field in enumerate(columns):
        zero = jnp.zeros_like(field[:1])
        above = jnp.concatenate([zero, field[:-1]], axis=0)
        below = jnp.concatenate([field[1:], zero], axis=0)
        total = total + (
            k_ref[index, 0, j : j + 1, :] * above
            + k_ref[index, 1, j : j + 1, :] * field
            + k_ref[index, 2, j : j + 1, :] * below
        )
    return total


def ocean_kernel(scale_ref, own_ref, pair_ref, next_ref, k_ref, point_ref, gain_ref, qkv_ref,
                 out_ref, last_ref, field_ref, pool_ref, wide_ref, merged_ref):
    mean_matrix = head_mean(128)
    row = lax.broadcasted_iota(jnp.int32, (128, 128), 0) % 8
    col = lax.broadcasted_iota(jnp.int32, (128, 128), 1) % 8
    mask = jnp.where(row == col, 1.0, 0.0)
    first_of_pair = (lax.axis_index("lat") + lax.axis_index("comp")) % 2 == 0
    fine_all = []
    for m in range(2):
        def rows_of(ref):
            even = ref[:, 2 * m].astype(F32)[:, None]
            odd = ref[:, 2 * m + 1].astype(F32)[:, None]
            return jnp.concatenate([even, odd], axis=1).reshape(32, 8, OCEAN)

        pair = rows_of(pair_ref)
        following = rows_of(next_ref)
        field_ref[m, :, 0:8, :] = jnp.where(first_of_pair, following, pair)
        field_ref[m, :, 8:16, :] = rows_of(own_ref)
        field_ref[m, :, 16:24, :] = jnp.where(first_of_pair, pair, following)
        act = taps3([field_ref[m, :, 3 + j : 19 + j, :] for j in range(3)], k_ref, 0)
        act = act.astype(BF16).reshape(32 * 16, OCEAN)
        fine = gelu(dot(act, point_ref[0])).astype(BF16).astype(F32).reshape(16, 2, 16, OCEAN)
        fine_all.append(fine)
        pool_ref[m] = (fine[:, 0] + fine[:, 1]).reshape(256, OCEAN)
    coarse = []
    for m in range(2):
        pooled = pool_ref[m, pl.ds(0, 128, stride=2), :] + pool_ref[m, pl.ds(1, 128, stride=2), :]
        coarse.append((pooled * 0.25).astype(BF16).astype(F32).reshape(16, 8, OCEAN))
    acts = []
    for m in range(2):
        columns = (shift_cols(coarse[m], 1, 1), coarse[m], shift_cols(coarse[m], -1, 1))
        acts.append(taps3(columns, k_ref, 1).astype(BF16).reshape(128, OCEAN))
    first = gelu(dot(jnp.concatenate(acts, axis=0), point_ref[1])).astype(BF16).astype(F32)
    normed = norm_rows(first, gain_ref[...]).astype(BF16)
    qkv = dot(normed, qkv_ref[...])
    query = unit(qkv[:, :128], mean_matrix)
    key = unit(qkv[:, 128:256], mean_matrix)
    value = qkv[:, 256:].astype(BF16)
    attended = []
    for m in range(2):
        at = slice(128 * m, 128 * m + 128)
        attended.append(
            pair_attend(
                query[at],
                key[at],
                value[at],
                mask,
                scale_ref[:, 0:1] * (LOG2E / 64),
                scale_ref[:, 1:2] * (LOG2E / 64),
            )
        )
    attended = jnp.concatenate(attended, axis=0)
    coarse_next = (first + dot(attended, out_ref[...])).astype(BF16).astype(F32)
    for m in range(2):
        piece = coarse_next[128 * m : 128 * m + 128]
        wide_ref[m, pl.ds(0, 128, stride=2), :] = piece
        wide_ref[m, pl.ds(1, 128, stride=2), :] = piece
    for m in range(2):
        spread = wide_ref[m].reshape(16, 1, 16, OCEAN)
        merged_ref[m] = (fine_all[m] + spread).astype(BF16).astype(F32).reshape(32, 16, OCEAN)
        act = taps3([merged_ref[m, :, 3 + j : 11 + j, :] for j in range(3)], k_ref, 2)
        act = act.astype(BF16).reshape(16, 2, 8, OCEAN)
        last_ref[:, 2 * m] = act[:, 0]
        last_ref[:, 2 * m + 1] = act[:, 1]


def ocean_call(*args):
    return pl.pallas_call(
        ocean_kernel,
        out_shape=pltpu.VMEM((16, 4, 8, OCEAN), BF16),
        in_specs=[VM] * 9,
        out_specs=VM,
        compiler_params=BLOCK_PARAMS,
        scratch_shapes=[
            pltpu.VMEM((2, 32, 24, OCEAN), F32),
            pltpu.VMEM((2, 256, OCEAN), F32),
            pltpu.VMEM((2, 256, OCEAN), F32),
            pltpu.VMEM((2, 32, 16, OCEAN), F32),
        ],
        name="ocean",
    )(*near(*args))


def final_kernel(last_ref, start_ref, cur_ref, sea_ref, point_ref, return_ref, air_hbm, water_hbm,
                 air_ref, water_ref, sems):
    copies = []

    def send(src, dst, m, r, k):
        copies.append(pltpu.make_async_copy(src.at[m, r], dst.at[m, r], sems.at[k]))
        copies[-1].start()

    straight = lax.axis_index("comp") == 0
    acts = [
        turned(last_ref[:, i].astype(F32), straight).astype(BF16).reshape(COLS, OCEAN) for i in range(4)
    ]
    lifted = gelu(dot(jnp.concatenate(acts, axis=0), point_ref[2]))
    waters = []
    for i in range(4):
        m, r = i // 2, i % 2
        start = turned(start_ref[:, i].astype(F32), straight).reshape(COLS, OCEAN)
        waters.append((sea_ref[r] * (start + lifted[COLS * i : COLS * i + COLS])).astype(BF16))
        water_ref[m, r] = waters[i]
        send(water_ref, water_hbm, m, r, i)
    back = dot(jnp.concatenate(waters, axis=0), return_ref[...])
    for i in range(4):
        m, r = i // 2, i % 2
        sea = jnp.concatenate([sea_ref[r]] * 3, axis=1)
        air_ref[m, r] = (cur_ref[m, r].astype(F32) + sea * back[COLS * i : COLS * i + COLS]).astype(BF16)
        send(air_ref, air_hbm, m, r, 4 + i)
    for copy in copies:
        copy.wait()


def final_call(*args):
    return pl.pallas_call(
        final_kernel,
        out_shape=(
            jax.ShapeDtypeStruct((2, 2, COLS, WIDTH), BF16),
            jax.ShapeDtypeStruct((2, 2, COLS, OCEAN), BF16),
        ),
        in_specs=[VM] * 6,
        out_specs=(ANY, ANY),
        scratch_shapes=[
            pltpu.VMEM((2, 2, COLS, WIDTH), BF16),
            pltpu.VMEM((2, 2, COLS, OCEAN), BF16),
            pltpu.SemaphoreType.DMA((8,)),
        ],
        compiler_params=PARAMS,
        name="final",
    )(*near(*args))


LON = ("lon", "comp")


def ring(count, step):
    return [(i, (i + step) % count) for i in range(count)]


def group_swap(first):
    lats = lax.axis_size("lat")
    sectors = lax.axis_size("lon") * lax.axis_size("comp")
    total = lats * sectors

    def device(g):
        sector, place = g // lats, g % lats
        lat = place if sector % 2 == 0 else lats - 1 - place
        return lat * sectors + sector

    pairs = []
    for g in range(first, total, 2):
        a, b = device(g), device((g + 1) % total)
        pairs += [(a, b), (b, a)]
    return sorted(pairs)


def mix(block, top, bot, kernels, gain, qkv, *after):
    lats = lax.axis_size("lat")
    sectors = lax.axis_size("lon") * lax.axis_size("comp")
    up = lax.ppermute(bot, "lat", ring(lats, 1))
    down = lax.ppermute(top, "lat", ring(lats, -1))
    mate, far = edge_call(block, top, bot, up, down, kernels, *after)
    far = lax.ppermute(far, LON, [(i, (i + 2 * (i % 2) - 1) % sectors) for i in range(sectors)])
    mate = lax.ppermute(mate, LON, [(i, i ^ 1) for i in range(sectors)])
    part = conv_call(block, top, bot, up, down, kernels, gain, qkv)
    return (*part, mate, far)


def start_copies(sources, targets, sems):
    copies = [
        pltpu.make_async_copy(src, dst, sems.at[i]) for i, (src, dst) in enumerate(zip(sources, targets))
    ]
    for copy in copies:
        copy.start()
    return copies


def load_kernel(block, count, *refs):
    sources = [
        ref if i < count - 4 else ref.at[block] for i, ref in enumerate(refs[:count])
    ]
    if block == 0:
        mask_ref, sea_ref = refs[count : count + 2]
        ids_ref, land_ref, sems = refs[-3:]
        targets = (ids_ref, land_ref) + tuple(refs[count + 2 : -3])
        copies = start_copies(sources, targets, sems)
        for copy in copies[:2]:
            copy.wait()
        for r in range(2):
            ids = jnp.broadcast_to(ids_ref[r : r + 1, :].astype(F32), (COLS, COLS))
            mask_ref[r] = (ids == ids.T).astype(F32)
            sea_ref[r] = jnp.broadcast_to(land_ref[r : r + 1, :].astype(F32), (COLS, COLS)).T
        copies = copies[2:]
    else:
        copies = start_copies(sources, refs[count:-1], refs[-1])
    for copy in copies:
        copy.wait()


def split_kernel(state_ref, top_ref, bot_ref, sems):
    copies = [
        pltpu.make_async_copy(state_ref.at[m, r], ref.at[m], sems.at[2 * r + m])
        for r, ref in ((1, bot_ref), (0, top_ref))
        for m in range(2)
    ]
    for copy in copies:
        copy.start()
    for copy in copies:
        copy.wait()


def split_call(state):
    row = pltpu.VMEM((2, COLS, WIDTH), BF16)
    return pl.pallas_call(
        split_kernel,
        out_shape=(row, row),
        in_specs=[ANY],
        out_specs=(VM, VM),
        scratch_shapes=[pltpu.SemaphoreType.DMA((4,))],
        compiler_params=PARAMS,
        name="split",
    )(pltpu.with_memory_space_constraint(state, pltpu.HBM))


def load_call(block, *arrays):
    count = len(arrays)
    shapes = [a.shape for a in arrays[:-4]] + [a.shape[1:] for a in arrays[-4:]]
    outs = [pltpu.VMEM(s, a.dtype) for s, a in zip(shapes, arrays)]
    scratch = [pltpu.SemaphoreType.DMA((count,))]
    if block == 0:
        outs = [pltpu.VMEM((2, COLS, COLS), F32)] * 2 + outs[2:]
        scratch = [pltpu.VMEM((2, COLS), jnp.int32), pltpu.VMEM((2, COLS), jnp.int32)] + scratch
    return pl.pallas_call(
        lambda *refs: load_kernel(block, count, *refs),
        out_shape=outs,
        in_specs=[ANY] * count,
        out_specs=[VM] * len(outs),
        scratch_shapes=scratch,
        compiler_params=PARAMS,
    )(*(pltpu.with_memory_space_constraint(a, pltpu.HBM) for a in arrays))


def per_device(atm_state, ocean_prev, land_sea, window_ids, conv_atm, attn_gain, qkv_matrix,
               attn_scales, out_matrix, mlp_gain, member_in, member_out, up_matrix, down_matrix,
               flux_matrix, conv_ocean, point_matrix, ocean_gain, ocean_qkv, ocean_scale, ocean_out,
               seaside_return_matrix):
    big = (qkv_matrix, out_matrix, up_matrix, down_matrix)
    mask, sea, conv_atm, attn_scales, attn_gain, mlp_gain, member_in, member_out, *weights = load_call(
        0, window_ids, land_sea, jnp.transpose(conv_atm, (1, 2, 0, 3)), attn_scales, attn_gain,
        mlp_gain, member_in, member_out, *big
    )
    small = (attn_gain, mlp_gain, member_in, member_out)
    mixed = mix(0, *split_call(atm_state), conv_atm, attn_gain, weights[0])
    top, bot = first_call(attn_scales, *mixed, mask, *small, *weights)

    (ocean_prev, flux_matrix, conv_ocean, point_matrix, ocean_gain, ocean_qkv, ocean_scale, ocean_out,
     seaside_return_matrix, *weights) = load_call(
        1, ocean_prev, flux_matrix, conv_ocean, point_matrix, ocean_gain[None, :], ocean_qkv,
        ocean_scale[None, :], ocean_out, seaside_return_matrix, *big
    )
    mixed = mix(1, top, bot, conv_atm, attn_gain, weights[0], ocean_scale)
    current, start = second_call(
        attn_scales, *mixed, mask, *small, *weights, ocean_prev, sea, flux_matrix
    )
    own = lax.all_to_all(start, "lat", 0, 0)
    axes = ("lat",) + LON
    pair = lax.ppermute(own, axes, group_swap(0))
    following = lax.ppermute(own, axes, group_swap(1))
    last = ocean_call(ocean_scale, own, pair, following, conv_ocean, point_matrix,
                      ocean_gain, ocean_qkv, ocean_out)
    last = lax.all_to_all(last, "lat", 0, 0)
    return final_call(last, start, current, sea, point_matrix, seaside_return_matrix)


def solution(mesh):
    field = P(None, "lat", LON, None)
    column = P("lat", LON)
    return jax.shard_map(
        per_device,
        mesh=mesh,
        in_specs=(field, field, column, column) + (P(),) * 18,
        out_specs=(field, field),
        check_vma=False,
    )
```
